256 devices in a mesh: rows: 32 (over z, x), cols: 8 (over y, core).
Axes of the slice: x: 4, y: 4, z: 8, core: 2. Of those that a mesh axis runs over, the one named last changes fastest.
Arguments:
- panel_t: float32 [16, 16384], P(None, ('rows', 'cols')), may hold values from -6 to 6
- kinship: float32 [16384, 16384], P('rows', 'cols'), may hold values from -0.046875 to 0.046875
Outputs:
- kin_panel_t: float32 [16, 16384], P(None, ('rows', 'cols'))
- score: float32 [16, 16], replicated
The draws below stay inside these ranges and needn't reach their ends.
All inputs are finite; a program needn't handle non-finite values.
Results may differ from the reference program's by a relative error of at most 0.00008.
Values sent between devices are 32-bit elements; how exact they have to be, the bound alone decides.
No kernel may reach another device: no remote copies, remote signals or barrier semaphores. Data moves between devices by JAX's collectives and lax.ppermute only.
A program may use at most 64 MiB of HBM per device.

```python
import jax
import jax.numpy as jnp
from jax import lax

TRAITS = 16
SAMPLES = 16384


def block_levels(rng, shape, pieces, smallest, largest):
    loudness, own = 1.0, jax.random.fold_in(rng, 6)
    for dim, parts in pieces:
        heights = jnp.exp(jax.random.uniform(jax.random.fold_in(own, dim), (parts,), jnp.float32, smallest / len(pieces), largest / len(pieces)))
        loudness = loudness * jnp.repeat(heights, shape[dim] // parts).reshape([-1 if axis == dim else 1 for axis in range(len(shape))])
    return loudness


def centred(key, shape, scale, most, pieces=(), dtype=jnp.bfloat16):
    factor_of = block_levels(key, shape, pieces, -0.22, 0.18) if pieces else 1.0
    drawn = jax.random.normal(key, shape, jnp.float32) * scale * factor_of
    return jnp.minimum(jnp.maximum(drawn, -most), most).astype(dtype)


def setup_inputs(seed: int = 0) -> dict:
    streams_of = jax.random.split(jax.random.key(seed), 3)
    panel_t = centred(streams_of[0], (TRAITS, SAMPLES), 1.0, 6.0, ((1, 256),), jnp.float32)
    kinship = centred(streams_of[1], (SAMPLES, SAMPLES), SAMPLES ** -0.5, 0.046875, ((0, 32), (1, 8)), jnp.float32)
    return dict(panel_t=panel_t, kinship=kinship)


def reference(panel_t, kinship):
    kin_panel_t = lax.dot_general(panel_t, kinship, (((1,), (1,)), ((), ())), precision=lax.Precision.HIGHEST, preferred_element_type=jnp.float32)
    score = lax.dot_general(panel_t, kin_panel_t, (((1,), (1,)), ((), ())), precision=lax.Precision.HIGHEST, preferred_element_type=jnp.float32)
    score = score / jnp.sqrt(jnp.float32(panel_t.shape[1]))
    return (kin_panel_t, score)
```

```python
import itertools

import jax
import jax.numpy as jnp
from jax import lax
from jax.experimental import pallas as pl
from jax.experimental.pallas import tpu as pltpu
from jax.sharding import Mesh
from jax.sharding import PartitionSpec as P

Z, X, Y, C = 8, 4, 4, 2
AXES = ("z", "x", "y", "c")
ROWS = ("z", "x")
COLS = ("y", "c")
PLANE = ("x", "y", "c")
TRAITS = 16
OWN = 64
CHUNKS = 8
HALF = 64
VMEM = pl.BlockSpec(memory_space=pltpu.VMEM)
SMALL = pltpu.CompilerParams(vmem_limit_bytes=2 << 20)
LARGE = pltpu.CompilerParams(vmem_limit_bytes=16 << 20)


def number(z, x, y, c):
    return ((z * X + x) * Y + y) * C + c


def apart(a, b, n):
    d = abs(a - b) % n
    return min(d, n - d)


def plane_to_column():
    pairs = []
    for plane in range(Z):
        y_to, c_to = divmod(plane, C)
        senders = sorted(itertools.product(range(Y), range(C)), key=lambda s: (-apart(s[0], y_to, Y), (s[0] - y_to) % Y, s[1] != c_to))
        planes = sorted(range(Z), key=lambda z: (apart(z, plane, Z), (z - plane) % Z))
        for x in range(X):
            for (y, c), z in zip(senders, planes):
                pairs.append((number(plane, x, y, c), number(z, x, y_to, c_to)))
    return pairs


def low_lanes(shape):
    return lax.broadcasted_iota(jnp.int32, shape, len(shape) - 1) < HALF


def unpacked(a, b):
    low = low_lanes(a.shape)
    top = jnp.where(low, a, pltpu.roll(b, HALF, 1))
    bottom = jnp.where(low, pltpu.roll(a, HALF, 1), b)
    return jnp.concatenate([top, bottom], axis=0)


def packed(tile):
    top, bottom = tile[:8], tile[8:]
    low = low_lanes(top.shape)
    return jnp.where(low, top, pltpu.roll(bottom, HALF, 1)), jnp.where(low, pltpu.roll(top, HALF, 1), bottom)


def split(x):
    high = x.astype(jnp.bfloat16)
    return high, (x - high.astype(jnp.float32)).astype(jnp.bfloat16)


def nt(left, right):
    return lax.dot_general(left, right, (((1,), (1,)), ((), ())), preferred_element_type=jnp.float32)


def nn(left, right):
    return lax.dot_general(left, right, (((1,), (0,)), ((), ())), preferred_element_type=jnp.float32)


def pack_kernel(panel_ref, out_ref):
    panel = panel_ref[...]
    piece = jnp.concatenate([panel[:8], panel[8:]], axis=1)
    out_ref[...] = jnp.broadcast_to(piece[None], out_ref.shape)


def prepare_kernel(x_ref, slab_ref, kinship_ref, high_ref, low_ref, buffer, sems):
    rows = kinship_ref.shape[0]
    height = rows // CHUNKS

    def copy(i):
        return pltpu.make_async_copy(kinship_ref.at[pl.ds(i * height, height)], buffer.at[i], sems.at[i])

    for i in range(CHUNKS):
        copy(i).start()
    start = x_ref[0] * (Y * C)
    own = jnp.concatenate([unpacked(slab_ref[start + j], slab_ref[start + j + 1]) for j in range(0, Y * C, 2)], axis=1)
    own = jnp.concatenate(split(own), axis=0)
    for i in range(CHUNKS):
        copy(i).wait()
        high, low = split(buffer[i])
        high_ref[pl.ds(i * height, height), :] = high
        low_ref[pl.ds(i * height, height), :] = low
    form = nn(own, high_ref[:rows, :]) + nn(own, low_ref[:rows, :])
    high, low = split(form[:TRAITS] + form[TRAITS:])
    high_ref[rows:, :] = jnp.concatenate([high] * 8, axis=0)
    low_ref[rows:, :] = jnp.concatenate([low] * 8, axis=0)


def product_kernel(block_ref, high_ref, low_ref, out_ref):
    columns = high_ref.shape[1]
    tiles = [unpacked(block_ref[j], block_ref[j + 1]) for j in range(0, columns // OWN, 2)]
    panel = jnp.concatenate(split(jnp.concatenate(tiles, axis=1)), axis=0)
    total = nt(panel, high_ref[...]) + nt(panel, low_ref[...])
    total = total[:TRAITS] + total[TRAITS:]
    wide = total[:, -128:]
    row = lax.broadcasted_iota(jnp.int32, wide.shape, 0) % 8
    lane = lax.broadcasted_iota(jnp.int32, wide.shape, 1) // TRAITS
    wide = jnp.where(row == lane, wide, 0.0)
    top = jnp.sum(wide[:8], axis=0, keepdims=True)
    bottom = jnp.sum(wide[8:], axis=0, keepdims=True)
    score = jnp.concatenate([top, bottom, jnp.zeros((6, 128), jnp.float32)], axis=0)
    for y in range(Y):
        pair = packed(total[:, y * 128 : (y + 1) * 128])
        for c in range(C):
            out_ref[y * C + c, :8, :] = pair[c]
            out_ref[y * C + c, 8:, :] = score


def own_kernel(parts_ref, kin_ref, score_ref):
    total = jnp.sum(parts_ref[...], axis=0)
    both = total[:8]
    kin_ref[:8, :] = both[:, :HALF]
    kin_ref[8:, :] = pltpu.roll(both, HALF, 1)[:, :HALF]
    score_ref[...] = jnp.broadcast_to(total[8:10][None], score_ref.shape)


def score_kernel(parts_ref, out_ref, *, scale):
    total = jnp.sum(parts_ref[...], axis=0)
    rows = [total[b // 8 : b // 8 + 1, b % 8 * TRAITS : (b % 8 + 1) * TRAITS] for b in range(TRAITS)]
    out_ref[...] = jnp.concatenate(rows, axis=0).T * scale


def shards(panel_t, kinship):
    f32 = jnp.float32
    slab_rows = kinship.shape[0]
    peers = X * Y * C
    pieces = pl.pallas_call(pack_kernel, out_shape=jax.ShapeDtypeStruct((peers, 8, 128), f32), in_specs=[VMEM], out_specs=VMEM, compiler_params=SMALL, name="pack")(panel_t)
    slab = lax.all_to_all(pieces, PLANE, 0, 0, tiled=True)
    block = lax.ppermute(slab, AXES, plane_to_column())
    x_index = lax.axis_index("x").reshape(1)
    extended = jax.ShapeDtypeStruct((slab_rows + 8 * TRAITS, kinship.shape[1]), jnp.bfloat16)
    high, low = pl.pallas_call(
        prepare_kernel,
        out_shape=(extended, extended),
        in_specs=[pl.BlockSpec(memory_space=pltpu.SMEM), VMEM, pl.BlockSpec(memory_space=pltpu.HBM)],
        out_specs=(VMEM, VMEM),
        scratch_shapes=[pltpu.VMEM((CHUNKS, slab_rows // CHUNKS, kinship.shape[1]), f32), pltpu.SemaphoreType.DMA((CHUNKS,))],
        compiler_params=LARGE,
        name="prepare",
    )(x_index, slab, kinship)
    parts = pl.pallas_call(
        product_kernel,
        out_shape=jax.ShapeDtypeStruct((Y * C, 16, 128), f32),
        in_specs=[VMEM, VMEM, VMEM],
        out_specs=VMEM,
        compiler_params=LARGE,
        name="product",
    )(block, high, low)
    parts = lax.all_to_all(parts, COLS, 0, 0, tiled=True)
    kin_panel_t, scores = pl.pallas_call(
        own_kernel,
        out_shape=(jax.ShapeDtypeStruct(panel_t.shape, f32), jax.ShapeDtypeStruct((Z * X, 2, 128), f32)),
        in_specs=[VMEM],
        out_specs=(VMEM, VMEM),
        compiler_params=SMALL,
        name="own",
    )(parts)
    scores = lax.all_to_all(scores, ROWS, 0, 0, tiled=True)
    samples = OWN * Z * X * Y * C
    score = pl.pallas_call(
        lambda parts_ref, out_ref: score_kernel(parts_ref, out_ref, scale=samples**-0.5),
        out_shape=jax.ShapeDtypeStruct((TRAITS, TRAITS), f32),
        in_specs=[VMEM],
        out_specs=VMEM,
        compiler_params=SMALL,
        name="score",
    )(scores)
    return kin_panel_t, score


def solution(mesh):
    torus = Mesh(mesh.devices.reshape(Z, X, Y, C), AXES)
    return jax.shard_map(
        shards,
        mesh=torus,
        in_specs=(P(None, AXES), P(ROWS, COLS)),
        out_specs=(P(None, AXES), P()),
        check_vma=False,
    )
```

```python
import itertools

import jax
import jax.numpy as jnp
from jax import lax
from jax.experimental import pallas as pl
from jax.experimental.pallas import tpu as pltpu
from jax.sharding import Mesh
from jax.sharding import PartitionSpec as P

Z, X, Y, C = 8, 4, 4, 2
AXES = ("z", "x", "y", "c")
ROWS = ("z", "x")
COLS = ("y", "c")
PLANE = ("x", "y", "c")
TRAITS = 16
OWN = 64
CHUNKS = 8
HALF = 64
VMEM = pl.BlockSpec(memory_space=pltpu.VMEM)
SMALL = pltpu.CompilerParams(vmem_limit_bytes=2 << 20)
LARGE = pltpu.CompilerParams(vmem_limit_bytes=16 << 20)
WHOLE = pltpu.CompilerParams(vmem_limit_bytes=48 << 20)


def number(z, x, y, c):
    return ((z * X + x) * Y + y) * C + c


def apart(a, b, n):
    d = abs(a - b) % n
    return min(d, n - d)


def plane_to_column():
    pairs = []
    for plane in range(Z):
        y_to, c_to = divmod(plane, C)
        senders = sorted(itertools.product(range(Y), range(C)), key=lambda s: (-apart(s[0], y_to, Y), (s[0] - y_to) % Y, s[1] != c_to))
        planes = sorted(range(Z), key=lambda z: (apart(z, plane, Z), (z - plane) % Z))
        for x in range(X):
            for (y, c), z in zip(senders, planes):
                pairs.append((number(plane, x, y, c), number(z, x, y_to, c_to)))
    return pairs


def low_lanes(shape):
    return lax.broadcasted_iota(jnp.int32, shape, len(shape) - 1) < HALF


def unpacked(a, b):
    low = low_lanes(a.shape)
    top = jnp.where(low, a, pltpu.roll(b, HALF, 1))
    bottom = jnp.where(low, pltpu.roll(a, HALF, 1), b)
    return jnp.concatenate([top, bottom], axis=0)


def packed(tile):
    top, bottom = tile[:8], tile[8:]
    low = low_lanes(top.shape)
    return jnp.where(low, top, pltpu.roll(bottom, HALF, 1)), jnp.where(low, pltpu.roll(top, HALF, 1), bottom)


def split(x):
    high = x.astype(jnp.bfloat16)
    return high, (x - high.astype(jnp.float32)).astype(jnp.bfloat16)


def nt(left, right):
    return lax.dot_general(left, right, (((1,), (1,)), ((), ())), preferred_element_type=jnp.float32)


def nn(left, right):
    return lax.dot_general(left, right, (((1,), (0,)), ((), ())), preferred_element_type=jnp.float32)


def pack_kernel(panel_ref, out_ref):
    panel = panel_ref[...]
    piece = jnp.concatenate([panel[:8], panel[8:]], axis=1)
    out_ref[...] = jnp.broadcast_to(piece[None], out_ref.shape)


def prepare_kernel(x_ref, slab_ref, kinship_ref, high_ref, low_ref, buffer, sems):
    rows = kinship_ref.shape[0]
    height = rows // CHUNKS

    def copy(i):
        return pltpu.make_async_copy(kinship_ref.at[pl.ds(i * height, height)], buffer.at[i], sems.at[i])

    for i in range(CHUNKS):
        copy(i).start()
    start = x_ref[0] * (Y * C)
    own = jnp.concatenate([unpacked(slab_ref[start + j], slab_ref[start + j + 1]) for j in range(0, Y * C, 2)], axis=1)
    own = jnp.concatenate(split(own), axis=0)
    for i in range(CHUNKS):
        copy(i).wait()
        high, low = split(buffer[i])
        high_ref[pl.ds(i * height, height), :] = high
        low_ref[pl.ds(i * height, height), :] = low
    form = nn(own, high_ref[:rows, :]) + nn(own, low_ref[:rows, :])
    high, low = split(form[:TRAITS] + form[TRAITS:])
    high_ref[rows:, :] = jnp.concatenate([high] * 4 + [low] * 4, axis=0)


def product_kernel(block_ref, high_ref, low_ref, out_ref):
    columns = high_ref.shape[1]
    tiles = [unpacked(block_ref[j], block_ref[j + 1]) for j in range(0, columns // OWN, 2)]
    panel = jnp.concatenate(split(jnp.concatenate(tiles, axis=1)), axis=0)
    rows = low_ref.shape[0]
    first = nt(panel, high_ref[...])
    total = first[:, :rows] + nt(panel, low_ref[...])
    total = total[:TRAITS] + total[TRAITS:]
    wide = first[:TRAITS, rows:] + first[TRAITS:, rows:]
    wide = wide + pltpu.roll(wide, HALF, 1)
    row = lax.broadcasted_iota(jnp.int32, wide.shape, 0) % 8
    lane = lax.broadcasted_iota(jnp.int32, wide.shape, 1) // TRAITS
    wide = jnp.where(row == lane, wide, 0.0)
    top = jnp.sum(wide[:8], axis=0, keepdims=True)
    bottom = jnp.sum(wide[8:], axis=0, keepdims=True)
    score = jnp.concatenate([top, bottom, jnp.zeros((6, 128), jnp.float32)], axis=0)
    for y in range(Y):
        pair = packed(total[:, y * 128 : (y + 1) * 128])
        for c in range(C):
            out_ref[y * C + c, :8, :] = pair[c]
            out_ref[y * C + c, 8:, :] = score


def own_kernel(parts_ref, own_ref, score_ref):
    total = jnp.sum(parts_ref[...], axis=0)
    own_ref[...] = total[:8]
    score_ref[...] = jnp.broadcast_to(total[8:10][None], score_ref.shape)


def result_kernel(own_ref, parts_ref, kin_ref, score_ref, *, scale):
    own = own_ref[...]
    kin_ref[:8, :] = own[:, :HALF]
    kin_ref[8:, :] = pltpu.roll(own, HALF, 1)[:, :HALF]
    total = jnp.sum(parts_ref[...], axis=0)
    rows = [total[b // 8 : b // 8 + 1, b % 8 * TRAITS : (b % 8 + 1) * TRAITS] for b in range(TRAITS)]
    score_ref[...] = jnp.concatenate(rows, axis=0).T * scale


def shards(panel_t, kinship):
    f32 = jnp.float32
    slab_rows = kinship.shape[0]
    peers = X * Y * C
    pieces = pl.pallas_call(pack_kernel, out_shape=jax.ShapeDtypeStruct((peers, 8, 128), f32), in_specs=[VMEM], out_specs=VMEM, compiler_params=SMALL, name="pack")(panel_t)
    slab = lax.all_to_all(pieces, PLANE, 0, 0, tiled=True)
    block = lax.ppermute(slab, AXES, plane_to_column())
    x_index = lax.axis_index("x").reshape(1)
    high, low = pl.pallas_call(
        prepare_kernel,
        out_shape=(
            jax.ShapeDtypeStruct((slab_rows + 8 * TRAITS, kinship.shape[1]), jnp.bfloat16),
            jax.ShapeDtypeStruct(kinship.shape, jnp.bfloat16),
        ),
        in_specs=[pl.BlockSpec(memory_space=pltpu.SMEM), VMEM, pl.BlockSpec(memory_space=pltpu.HBM)],
        out_specs=(VMEM, VMEM),
        scratch_shapes=[pltpu.VMEM((CHUNKS, slab_rows // CHUNKS, kinship.shape[1]), f32), pltpu.SemaphoreType.DMA((CHUNKS,))],
        compiler_params=WHOLE,
        name="prepare",
    )(x_index, slab, kinship)
    parts = pl.pallas_call(
        product_kernel,
        out_shape=jax.ShapeDtypeStruct((Y * C, 16, 128), f32),
        in_specs=[VMEM, VMEM, VMEM],
        out_specs=VMEM,
        compiler_params=LARGE,
        name="product",
    )(block, high, low)
    parts = lax.all_to_all(parts, COLS, 0, 0, tiled=True)
    own, scores = pl.pallas_call(
        own_kernel,
        out_shape=(jax.ShapeDtypeStruct((8, 128), f32), jax.ShapeDtypeStruct((Z * X, 2, 128), f32)),
        in_specs=[VMEM],
        out_specs=(VMEM, VMEM),
        compiler_params=SMALL,
        name="own",
    )(parts)
    scores = lax.all_to_all(scores, ROWS, 0, 0, tiled=True)
    samples = OWN * Z * X * Y * C
    return pl.pallas_call(
        lambda *refs: result_kernel(*refs, scale=samples**-0.5),
        out_shape=(jax.ShapeDtypeStruct(panel_t.shape, f32), jax.ShapeDtypeStruct((TRAITS, TRAITS), f32)),
        in_specs=[VMEM, VMEM],
        out_specs=(VMEM, VMEM),
        compiler_params=SMALL,
        name="result",
    )(own, scores)


def solution(mesh):
    torus = Mesh(mesh.devices.reshape(Z, X, Y, C), AXES)
    return jax.shard_map(
        shards,
        mesh=torus,
        in_specs=(P(None, AXES), P(ROWS, COLS)),
        out_specs=(P(None, AXES), P()),
        check_vma=False,
    )
```

```python
import itertools

import jax
import jax.numpy as jnp
from jax import lax
from jax.experimental import pallas as pl
from jax.experimental.pallas import tpu as pltpu
from jax.sharding import Mesh
from jax.sharding import PartitionSpec as P

Z, X, Y, C = 8, 4, 4, 2
AXES = ("z", "x", "y", "c")
ROWS = ("z", "x")
COLS = ("y", "c")
PLANE = ("x", "y", "c")
TRAITS = 16
OWN = 64
CHUNKS = 8
HALF = 64
VMEM = pl.BlockSpec(memory_space=pltpu.VMEM)
SMALL = pltpu.CompilerParams(vmem_limit_bytes=2 << 20)
LARGE = pltpu.CompilerParams(vmem_limit_bytes=16 << 20)
WHOLE = pltpu.CompilerParams(vmem_limit_bytes=48 << 20)


def number(z, x, y, c):
    return ((z * X + x) * Y + y) * C + c


def apart(a, b, n):
    d = abs(a - b) % n
    return min(d, n - d)


def plane_to_column():
    pairs = []
    for plane in range(Z):
        y_to, c_to = divmod(plane, C)
        senders = sorted(itertools.product(range(Y), range(C)), key=lambda s: (-apart(s[0], y_to, Y), (s[0] - y_to) % Y, s[1] != c_to))
        planes = sorted(range(Z), key=lambda z: (apart(z, plane, Z), (z - plane) % Z))
        for x in range(X):
            for (y, c), z in zip(senders, planes):
                pairs.append((number(plane, x, y, c), number(z, x, y_to, c_to)))
    return pairs


def low_lanes(shape):
    return lax.broadcasted_iota(jnp.int32, shape, len(shape) - 1) < HALF


def unpacked(a, b):
    low = low_lanes(a.shape)
    top = jnp.where(low, a, pltpu.roll(b, HALF, 1))
    bottom = jnp.where(low, pltpu.roll(a, HALF, 1), b)
    return jnp.concatenate([top, bottom], axis=0)


def packed(tile):
    top, bottom = tile[:8], tile[8:]
    low = low_lanes(top.shape)
    return jnp.where(low, top, pltpu.roll(bottom, HALF, 1)), jnp.where(low, pltpu.roll(top, HALF, 1), bottom)


def split(x):
    high = x.astype(jnp.bfloat16)
    return high, (x - high.astype(jnp.float32)).astype(jnp.bfloat16)


def nt(left, right):
    return lax.dot_general(left, right, (((1,), (1,)), ((), ())), preferred_element_type=jnp.float32)


def nn(left, right):
    return lax.dot_general(left, right, (((1,), (0,)), ((), ())), preferred_element_type=jnp.float32)


def pack_kernel(panel_ref, out_ref):
    panel = panel_ref[...]
    piece = jnp.concatenate([panel[:8], panel[8:]], axis=1)
    out_ref[...] = jnp.broadcast_to(piece[None], out_ref.shape)


def prepare_kernel(x_ref, slab_ref, kinship_ref, high_ref, low_ref, buffer, sems):
    rows = kinship_ref.shape[0]
    height = rows // CHUNKS

    def copy(i):
        return pltpu.make_async_copy(kinship_ref.at[pl.ds(i * height, height)], buffer.at[i], sems.at[i])

    for i in range(CHUNKS):
        copy(i).start()
    start = x_ref[0] * (Y * C)
    own = jnp.concatenate([unpacked(slab_ref[start + j], slab_ref[start + j + 1]) for j in range(0, Y * C, 2)], axis=1)
    own = jnp.concatenate(split(own), axis=0)
    for i in range(CHUNKS):
        copy(i).wait()
        high, low = split(buffer[i])
        high_ref[pl.ds(i * height, height), :] = high
        low_ref[pl.ds(i * height, height), :] = low
    form = nn(own, high_ref[:rows, :]) + nn(own, low_ref[:rows, :])
    high, low = split(form[:TRAITS] + form[TRAITS:])
    high_ref[rows:, :] = jnp.concatenate([high] * 4 + [low] * 4, axis=0)


def half_product(block_ref, high_ref, low_ref, start):
    columns = block_ref.shape[0] * OWN
    tiles = [unpacked(block_ref[j], block_ref[j + 1]) for j in range(0, block_ref.shape[0], 2)]
    panel = jnp.concatenate(split(jnp.concatenate(tiles, axis=1)), axis=0)
    rows = low_ref.shape[0]
    both = nt(panel, high_ref[:, start : start + columns])
    partial = both[:, :rows] + nt(panel, low_ref[:, start : start + columns])
    return partial[:TRAITS] + partial[TRAITS:], both[:TRAITS, rows:] + both[TRAITS:, rows:]


def first_kernel(block_ref, high_ref, low_ref, partial_ref, wide_ref):
    partial_ref[...], wide_ref[...] = half_product(block_ref, high_ref, low_ref, 0)


def second_kernel(block_ref, high_ref, low_ref, partial_ref, wide_ref, out_ref):
    total, wide = half_product(block_ref, high_ref, low_ref, block_ref.shape[0] * OWN)
    total = total + partial_ref[...]
    wide = wide + wide_ref[...]
    wide = wide + pltpu.roll(wide, HALF, 1)
    row = lax.broadcasted_iota(jnp.int32, wide.shape, 0) % 8
    lane = lax.broadcasted_iota(jnp.int32, wide.shape, 1) // TRAITS
    wide = jnp.where(row == lane, wide, 0.0)
    top = jnp.sum(wide[:8], axis=0, keepdims=True)
    bottom = jnp.sum(wide[8:], axis=0, keepdims=True)
    score = jnp.concatenate([top, bottom, jnp.zeros((6, 128), jnp.float32)], axis=0)
    for y in range(Y):
        pair = packed(total[:, y * 128 : (y + 1) * 128])
        for c in range(C):
            out_ref[y * C + c, :8, :] = pair[c]
            out_ref[y * C + c, 8:, :] = score


def own_kernel(parts_ref, own_ref, score_ref):
    total = jnp.sum(parts_ref[...], axis=0)
    own_ref[...] = total[:8]
    score_ref[...] = jnp.broadcast_to(total[8:10][None], score_ref.shape)


def result_kernel(own_ref, parts_ref, kin_ref, score_ref, *, scale):
    own = own_ref[...]
    kin_ref[:8, :] = own[:, :HALF]
    kin_ref[8:, :] = pltpu.roll(own, HALF, 1)[:, :HALF]
    total = jnp.sum(parts_ref[...], axis=0)
    rows = [total[b // 8 : b // 8 + 1, b % 8 * TRAITS : (b % 8 + 1) * TRAITS] for b in range(TRAITS)]
    score_ref[...] = jnp.concatenate(rows, axis=0).T * scale


def shards(panel_t, kinship):
    f32 = jnp.float32
    slab_rows = kinship.shape[0]
    peers = X * Y * C
    pieces = pl.pallas_call(pack_kernel, out_shape=jax.ShapeDtypeStruct((peers, 8, 128), f32), in_specs=[VMEM], out_specs=VMEM, compiler_params=SMALL, name="pack")(panel_t)
    slab = lax.all_to_all(pieces, PLANE, 0, 0, tiled=True)
    pairs = plane_to_column()
    early = lax.ppermute(slab[: peers // 2], AXES, pairs)
    late = lax.ppermute(slab[peers // 2 :], AXES, pairs)
    x_index = lax.axis_index("x").reshape(1)
    high, low = pl.pallas_call(
        prepare_kernel,
        out_shape=(
            jax.ShapeDtypeStruct((slab_rows + 8 * TRAITS, kinship.shape[1]), jnp.bfloat16),
            jax.ShapeDtypeStruct(kinship.shape, jnp.bfloat16),
        ),
        in_specs=[pl.BlockSpec(memory_space=pltpu.SMEM), VMEM, pl.BlockSpec(memory_space=pltpu.HBM)],
        out_specs=(VMEM, VMEM),
        scratch_shapes=[pltpu.VMEM((CHUNKS, slab_rows // CHUNKS, kinship.shape[1]), f32), pltpu.SemaphoreType.DMA((CHUNKS,))],
        compiler_params=WHOLE,
        name="prepare",
    )(x_index, slab, kinship)
    partial, wide = pl.pallas_call(
        first_kernel,
        out_shape=(jax.ShapeDtypeStruct((TRAITS, slab_rows), f32), jax.ShapeDtypeStruct((TRAITS, 8 * TRAITS), f32)),
        in_specs=[VMEM, VMEM, VMEM],
        out_specs=(VMEM, VMEM),
        compiler_params=LARGE,
        name="first",
    )(early, high, low)
    parts = pl.pallas_call(
        second_kernel,
        out_shape=jax.ShapeDtypeStruct((Y * C, 16, 128), f32),
        in_specs=[VMEM] * 5,
        out_specs=VMEM,
        compiler_params=LARGE,
        name="second",
    )(late, high, low, partial, wide)
    parts = lax.all_to_all(parts, COLS, 0, 0, tiled=True)
    own, scores = pl.pallas_call(
        own_kernel,
        out_shape=(jax.ShapeDtypeStruct((8, 128), f32), jax.ShapeDtypeStruct((Z * X, 2, 128), f32)),
        in_specs=[VMEM],
        out_specs=(VMEM, VMEM),
        compiler_params=SMALL,
        name="own",
    )(parts)
    scores = lax.all_to_all(scores, ROWS, 0, 0, tiled=True)
    samples = OWN * Z * X * Y * C
    return pl.pallas_call(
        lambda *refs: result_kernel(*refs, scale=samples**-0.5),
        out_shape=(jax.ShapeDtypeStruct(panel_t.shape, f32), jax.ShapeDtypeStruct((TRAITS, TRAITS), f32)),
        in_specs=[VMEM, VMEM],
        out_specs=(VMEM, VMEM),
        compiler_params=SMALL,
        name="result",
    )(own, scores)


def solution(mesh):
    torus = Mesh(mesh.devices.reshape(Z, X, Y, C), AXES)
    return jax.shard_map(
        shards,
        mesh=torus,
        in_specs=(P(None, AXES), P(ROWS, COLS)),
        out_specs=(P(None, AXES), P()),
        check_vma=False,
    )
```

```python
import itertools

import jax
import jax.numpy as jnp
from jax import lax
from jax.experimental import pallas as pl
from jax.experimental.pallas import tpu as pltpu
from jax.sharding import Mesh
from jax.sharding import PartitionSpec as P

Z, X, Y, C = 8, 4, 4, 2
AXES = ("z", "x", "y", "c")
ROWS = ("z", "x")
COLS = ("y", "c")
PLANE = ("x", "y", "c")
TRAITS = 16
OWN = 64
CHUNKS = 8
HALF = 64
VMEM = pl.BlockSpec(memory_space=pltpu.VMEM)
SMALL = pltpu.CompilerParams(vmem_limit_bytes=2 << 20)
LARGE = pltpu.CompilerParams(vmem_limit_bytes=16 << 20)
WHOLE = pltpu.CompilerParams(vmem_limit_bytes=48 << 20)


def number(z, x, y, c):
    return ((z * X + x) * Y + y) * C + c


def apart(a, b, n):
    d = abs(a - b) % n
    return min(d, n - d)


def plane_to_column():
    pairs = []
    for plane in range(Z):
        y_to, c_to = divmod(plane, C)
        senders = sorted(itertools.product(range(Y), range(C)), key=lambda s: (-apart(s[0], y_to, Y), (s[0] - y_to) % Y, s[1] != c_to))
        planes = sorted(range(Z), key=lambda z: (apart(z, plane, Z), (z - plane) % Z))
        for x in range(X):
            for (y, c), z in zip(senders, planes):
                pairs.append((number(plane, x, y, c), number(z, x, y_to, c_to)))
    return pairs


def low_lanes(shape):
    return lax.broadcasted_iota(jnp.int32, shape, len(shape) - 1) < HALF


def unpacked(a, b):
    low = low_lanes(a.shape)
    top = jnp.where(low, a, pltpu.roll(b, HALF, 1))
    bottom = jnp.where(low, pltpu.roll(a, HALF, 1), b)
    return jnp.concatenate([top, bottom], axis=0)


def packed(tile):
    top, bottom = tile[:8], tile[8:]
    low = low_lanes(top.shape)
    return jnp.where(low, top, pltpu.roll(bottom, HALF, 1)), jnp.where(low, pltpu.roll(top, HALF, 1), bottom)


def split(x):
    high = x.astype(jnp.bfloat16)
    return high, (x - high.astype(jnp.float32)).astype(jnp.bfloat16)


def nt(left, right):
    return lax.dot_general(left, right, (((1,), (1,)), ((), ())), preferred_element_type=jnp.float32)


def nn(left, right):
    return lax.dot_general(left, right, (((1,), (0,)), ((), ())), preferred_element_type=jnp.float32)


def pack_kernel(panel_ref, out_ref):
    panel = panel_ref[...]
    piece = jnp.concatenate([panel[:8], panel[8:]], axis=1)
    out_ref[...] = jnp.broadcast_to(piece[None], out_ref.shape)


def prepare_kernel(slab_ref, kinship_ref, high_ref, low_ref, late_ref, buffer, sems):
    rows = kinship_ref.shape[0]
    height = rows // CHUNKS

    def copy(i):
        return pltpu.make_async_copy(kinship_ref.at[pl.ds(i * height, height)], buffer.at[i], sems.at[i])

    for i in range(CHUNKS):
        copy(i).start()
    late_ref[...] = slab_ref[slab_ref.shape[0] - late_ref.shape[0] :]
    start = lax.axis_index("x") * (Y * C)
    own = jnp.concatenate([unpacked(slab_ref[start + j], slab_ref[start + j + 1]) for j in range(0, Y * C, 2)], axis=1)
    own = jnp.concatenate(split(own), axis=0)
    for i in range(CHUNKS):
        copy(i).wait()
        high, low = split(buffer[i])
        high_ref[pl.ds(i * height, height), :] = high
        low_ref[pl.ds(i * height, height), :] = low
    form = nn(own, high_ref[:rows, :]) + nn(own, low_ref[:rows, :])
    high, low = split(form[:TRAITS] + form[TRAITS:])
    high_ref[rows:, :] = jnp.concatenate([high] * 4 + [low] * 4, axis=0)


def half_product(block_ref, high_ref, low_ref, start):
    columns = block_ref.shape[0] * OWN
    tiles = [unpacked(block_ref[j], block_ref[j + 1]) for j in range(0, block_ref.shape[0], 2)]
    panel = jnp.concatenate(split(jnp.concatenate(tiles, axis=1)), axis=0)
    rows = low_ref.shape[0]
    both = nt(panel, high_ref[:, start : start + columns])
    partial = both[:, :rows] + nt(panel, low_ref[:, start : start + columns])
    return partial[:TRAITS] + partial[TRAITS:], both[:TRAITS, rows:] + both[TRAITS:, rows:]


def first_kernel(block_ref, high_ref, low_ref, partial_ref, wide_ref):
    partial_ref[...], wide_ref[...] = half_product(block_ref, high_ref, low_ref, 0)


def second_kernel(block_ref, high_ref, low_ref, partial_ref, wide_ref, out_ref):
    total, wide = half_product(block_ref, high_ref, low_ref, block_ref.shape[0] * OWN)
    total = total + partial_ref[...]
    wide = wide + wide_ref[...]
    wide = wide + pltpu.roll(wide, HALF, 1)
    row = lax.broadcasted_iota(jnp.int32, wide.shape, 0) % 8
    lane = lax.broadcasted_iota(jnp.int32, wide.shape, 1) // TRAITS
    wide = jnp.where(row == lane, wide, 0.0)
    top = jnp.sum(wide[:8], axis=0, keepdims=True)
    bottom = jnp.sum(wide[8:], axis=0, keepdims=True)
    score = jnp.concatenate([top, bottom, jnp.zeros((6, 128), jnp.float32)], axis=0)
    for y in range(Y):
        pair = packed(total[:, y * 128 : (y + 1) * 128])
        for c in range(C):
            out_ref[y * C + c, :8, :] = pair[c]
            out_ref[y * C + c, 8:, :] = score


def own_kernel(parts_ref, own_ref, score_ref):
    total = jnp.sum(parts_ref[...], axis=0)
    own_ref[...] = total[:8]
    score_ref[...] = jnp.broadcast_to(total[8:10][None], score_ref.shape)


def result_kernel(own_ref, parts_ref, kin_ref, score_ref, *, scale):
    own = own_ref[...]
    kin_ref[:8, :] = own[:, :HALF]
    kin_ref[8:, :] = pltpu.roll(own, HALF, 1)[:, :HALF]
    total = jnp.sum(parts_ref[...], axis=0)
    rows = [total[b // 8 : b // 8 + 1, b % 8 * TRAITS : (b % 8 + 1) * TRAITS] for b in range(TRAITS)]
    score_ref[...] = jnp.concatenate(rows, axis=0).T * scale


def shards(panel_t, kinship):
    f32 = jnp.float32
    slab_rows = kinship.shape[0]
    peers = X * Y * C
    pieces = pl.pallas_call(pack_kernel, out_shape=jax.ShapeDtypeStruct((peers, 8, 128), f32), in_specs=[VMEM], out_specs=VMEM, compiler_params=SMALL, name="pack")(panel_t)
    slab = lax.all_to_all(pieces, PLANE, 0, 0, tiled=True)
    pairs = plane_to_column()
    early = lax.ppermute(slab[: peers // 2], AXES, pairs)
    high, low, late = pl.pallas_call(
        prepare_kernel,
        out_shape=(
            jax.ShapeDtypeStruct((slab_rows + 8 * TRAITS, kinship.shape[1]), jnp.bfloat16),
            jax.ShapeDtypeStruct(kinship.shape, jnp.bfloat16),
            jax.ShapeDtypeStruct((peers // 2, 8, 128), f32),
        ),
        in_specs=[VMEM, pl.BlockSpec(memory_space=pltpu.HBM)],
        out_specs=(VMEM, VMEM, VMEM),
        scratch_shapes=[pltpu.VMEM((CHUNKS, slab_rows // CHUNKS, kinship.shape[1]), f32), pltpu.SemaphoreType.DMA((CHUNKS,))],
        compiler_params=WHOLE,
        name="prepare",
    )(slab, kinship)
    late = lax.ppermute(late, AXES, pairs)
    partial, wide = pl.pallas_call(
        first_kernel,
        out_shape=(jax.ShapeDtypeStruct((TRAITS, slab_rows), f32), jax.ShapeDtypeStruct((TRAITS, 8 * TRAITS), f32)),
        in_specs=[VMEM, VMEM, VMEM],
        out_specs=(VMEM, VMEM),
        compiler_params=LARGE,
        name="first",
    )(early, high, low)
    parts = pl.pallas_call(
        second_kernel,
        out_shape=jax.ShapeDtypeStruct((Y * C, 16, 128), f32),
        in_specs=[VMEM] * 5,
        out_specs=VMEM,
        compiler_params=LARGE,
        name="second",
    )(late, high, low, partial, wide)
    parts = lax.all_to_all(parts, COLS, 0, 0, tiled=True)
    own, scores = pl.pallas_call(
        own_kernel,
        out_shape=(jax.ShapeDtypeStruct((8, 128), f32), jax.ShapeDtypeStruct((Z * X, 2, 128), f32)),
        in_specs=[VMEM],
        out_specs=(VMEM, VMEM),
        compiler_params=SMALL,
        name="own",
    )(parts)
    scores = lax.all_to_all(scores, ROWS, 0, 0, tiled=True)
    samples = OWN * Z * X * Y * C
    return pl.pallas_call(
        lambda *refs: result_kernel(*refs, scale=samples**-0.5),
        out_shape=(jax.ShapeDtypeStruct(panel_t.shape, f32), jax.ShapeDtypeStruct((TRAITS, TRAITS), f32)),
        in_specs=[VMEM, VMEM],
        out_specs=(VMEM, VMEM),
        compiler_params=SMALL,
        name="result",
    )(own, scores)


def solution(mesh):
    torus = Mesh(mesh.devices.reshape(Z, X, Y, C), AXES)
    return jax.shard_map(
        shards,
        mesh=torus,
        in_specs=(P(None, AXES), P(ROWS, COLS)),
        out_specs=(P(None, AXES), P()),
        check_vma=False,
    )
```

```python
import itertools

import jax
import jax.numpy as jnp
from jax import lax
from jax.experimental import pallas as pl
from jax.experimental.pallas import tpu as pltpu
from jax.sharding import Mesh
from jax.sharding import PartitionSpec as P

Z, X, Y, C = 8, 4, 4, 2
AXES = ("z", "x", "y", "c")
ROWS = ("z", "x")
COLS = ("y", "c")
PLANE = ("x", "y", "c")
TRAITS = 16
OWN = 64
CHUNKS = 8
HALF = 64
VMEM = pl.BlockSpec(memory_space=pltpu.VMEM)
SMALL = pltpu.CompilerParams(vmem_limit_bytes=2 << 20)
LARGE = pltpu.CompilerParams(vmem_limit_bytes=16 << 20)
WHOLE = pltpu.CompilerParams(vmem_limit_bytes=48 << 20)


def number(z, x, y, c):
    return ((z * X + x) * Y + y) * C + c


def apart(a, b, n):
    d = abs(a - b) % n
    return min(d, n - d)


def plane_to_column():
    pairs = []
    for plane in range(Z):
        y_to, c_to = divmod(plane, C)
        senders = sorted(itertools.product(range(Y), range(C)), key=lambda s: (-apart(s[0], y_to, Y), (s[0] - y_to) % Y, s[1] != c_to))
        planes = sorted(range(Z), key=lambda z: (apart(z, plane, Z), (z - plane) % Z))
        for x in range(X):
            for (y, c), z in zip(senders, planes):
                pairs.append((number(plane, x, y, c), number(z, x, y_to, c_to)))
    return pairs


def low_lanes(shape):
    return lax.broadcasted_iota(jnp.int32, shape, len(shape) - 1) < HALF


def unpacked(a, b):
    low = low_lanes(a.shape)
    top = jnp.where(low, a, pltpu.roll(b, HALF, 1))
    bottom = jnp.where(low, pltpu.roll(a, HALF, 1), b)
    return jnp.concatenate([top, bottom], axis=0)


def packed(tile):
    top, bottom = tile[:8], tile[8:]
    low = low_lanes(top.shape)
    return jnp.where(low, top, pltpu.roll(bottom, HALF, 1)), jnp.where(low, pltpu.roll(top, HALF, 1), bottom)


def split(x):
    high = x.astype(jnp.bfloat16)
    return high, (x - high.astype(jnp.float32)).astype(jnp.bfloat16)


def nt(left, right):
    return lax.dot_general(left, right, (((1,), (1,)), ((), ())), preferred_element_type=jnp.float32)


def nn(left, right):
    return lax.dot_general(left, right, (((1,), (0,)), ((), ())), preferred_element_type=jnp.float32)


def pack_kernel(panel_ref, out_ref):
    panel = panel_ref[...]
    piece = jnp.concatenate([panel[:8], panel[8:]], axis=1)
    out_ref[...] = jnp.broadcast_to(piece[None], out_ref.shape)


def prepare_kernel(slab_ref, kinship_ref, high_ref, low_ref, form_ref, buffer, sems):
    rows = kinship_ref.shape[0]
    height = rows // CHUNKS

    def copy(i):
        return pltpu.make_async_copy(kinship_ref.at[pl.ds(i * height, height)], buffer.at[i], sems.at[i])

    for i in range(CHUNKS):
        copy(i).start()
    start = lax.axis_index("x") * (Y * C)
    own = jnp.concatenate([unpacked(slab_ref[start + j], slab_ref[start + j + 1]) for j in range(0, Y * C, 2)], axis=1)
    own = jnp.concatenate(split(own), axis=0)
    for i in range(CHUNKS):
        copy(i).wait()
        high, low = split(buffer[i])
        high_ref[pl.ds(i * height, height), :] = high
        low_ref[pl.ds(i * height, height), :] = low
    form = nn(own, high_ref[...]) + nn(own, low_ref[...])
    high, low = split(form[:TRAITS] + form[TRAITS:])
    form_ref[...] = jnp.concatenate([high] * 4 + [low] * 4, axis=0)


def panel_parts(early_ref, late_ref):
    refs = [ref.at[j : j + 2] for ref in (early_ref, late_ref) for j in range(0, ref.shape[0], 2)]
    return jnp.concatenate(split(jnp.concatenate([unpacked(ref[0], ref[1]) for ref in refs], axis=1)), axis=0)


def score_kernel(early_ref, late_ref, form_ref, out_ref):
    wide = nt(panel_parts(early_ref, late_ref), form_ref[...])
    wide = wide[:TRAITS] + wide[TRAITS:]
    wide = wide + pltpu.roll(wide, HALF, 1)
    row = lax.broadcasted_iota(jnp.int32, wide.shape, 0) % 8
    lane = lax.broadcasted_iota(jnp.int32, wide.shape, 1) // TRAITS
    wide = jnp.where(row == lane, wide, 0.0)
    top = jnp.sum(wide[:8], axis=0, keepdims=True)
    bottom = jnp.sum(wide[8:], axis=0, keepdims=True)
    out_ref[...] = jnp.broadcast_to(jnp.concatenate([top, bottom], axis=0)[None], out_ref.shape)


def product_kernel(early_ref, late_ref, high_ref, low_ref, out_ref):
    panel = panel_parts(early_ref, late_ref)
    total = nt(panel, high_ref[...]) + nt(panel, low_ref[...])
    total = total[:TRAITS] + total[TRAITS:]
    for y in range(Y):
        pair = packed(total[:, y * 128 : (y + 1) * 128])
        for c in range(C):
            out_ref[y * C + c] = pair[c]


def join_kernel(parts_ref, scores_ref, out_ref):
    out_ref[:, :8, :] = parts_ref[...]
    score = jnp.concatenate([jnp.sum(scores_ref[...], axis=0), jnp.zeros((6, 128), jnp.float32)], axis=0)
    out_ref[:, 8:, :] = jnp.broadcast_to(score[None], (out_ref.shape[0], 8, 128))


def result_kernel(parts_ref, kin_ref, score_ref, *, scale):
    total = jnp.sum(parts_ref[...], axis=0)
    own = total[:8]
    kin_ref[:8, :] = own[:, :HALF]
    kin_ref[8:, :] = pltpu.roll(own, HALF, 1)[:, :HALF]
    rows = [total[8 + b // 8 : 9 + b // 8, b % 8 * TRAITS : (b % 8 + 1) * TRAITS] for b in range(TRAITS)]
    score_ref[...] = jnp.concatenate(rows, axis=0).T * scale


def shards(panel_t, kinship):
    f32 = jnp.float32
    slab_rows = kinship.shape[0]
    peers = X * Y * C
    pieces = pl.pallas_call(pack_kernel, out_shape=jax.ShapeDtypeStruct((peers, 8, 128), f32), in_specs=[VMEM], out_specs=VMEM, compiler_params=SMALL, name="pack")(panel_t)
    slab = lax.all_to_all(pieces, PLANE, 0, 0, tiled=True)
    pairs = plane_to_column()
    early = lax.ppermute(slab[: peers // 2], AXES, pairs)
    late = lax.ppermute(slab[peers // 2 :], AXES, pairs)
    wide = jax.ShapeDtypeStruct((8 * TRAITS, kinship.shape[1]), jnp.bfloat16)
    half = jax.ShapeDtypeStruct(kinship.shape, jnp.bfloat16)
    high, low, form = pl.pallas_call(
        prepare_kernel,
        out_shape=(half, half, wide),
        in_specs=[VMEM, pl.BlockSpec(memory_space=pltpu.HBM)],
        out_specs=(VMEM, VMEM, VMEM),
        scratch_shapes=[pltpu.VMEM((CHUNKS, slab_rows // CHUNKS, kinship.shape[1]), f32), pltpu.SemaphoreType.DMA((CHUNKS,))],
        compiler_params=WHOLE,
        name="prepare",
    )(slab, kinship)
    scores = pl.pallas_call(
        score_kernel,
        out_shape=jax.ShapeDtypeStruct((Z * X, 2, 128), f32),
        in_specs=[VMEM] * 3,
        out_specs=VMEM,
        compiler_params=LARGE,
        name="score",
    )(early, late, form)
    scores = lax.all_to_all(scores, ROWS, 0, 0, tiled=True)
    parts = pl.pallas_call(
        product_kernel,
        out_shape=jax.ShapeDtypeStruct((Y * C, 8, 128), f32),
        in_specs=[VMEM] * 4,
        out_specs=VMEM,
        compiler_params=LARGE,
        name="product",
    )(early, late, high, low)
    parts = pl.pallas_call(
        join_kernel,
        out_shape=jax.ShapeDtypeStruct((Y * C, 16, 128), f32),
        in_specs=[VMEM] * 2,
        out_specs=VMEM,
        compiler_params=SMALL,
        name="join",
    )(parts, scores)
    parts = lax.all_to_all(parts, COLS, 0, 0, tiled=True)
    samples = OWN * Z * X * Y * C
    return pl.pallas_call(
        lambda *refs: result_kernel(*refs, scale=samples**-0.5),
        out_shape=(jax.ShapeDtypeStruct(panel_t.shape, f32), jax.ShapeDtypeStruct((TRAITS, TRAITS), f32)),
        in_specs=[VMEM],
        out_specs=(VMEM, VMEM),
        compiler_params=SMALL,
        name="result",
    )(parts)


def solution(mesh):
    torus = Mesh(mesh.devices.reshape(Z, X, Y, C), AXES)
    return jax.shard_map(
        shards,
        mesh=torus,
        in_specs=(P(None, AXES), P(ROWS, COLS)),
        out_specs=(P(None, AXES), P()),
        check_vma=False,
    )
```

```python
import jax
import jax.numpy as jnp
from jax import lax
from jax.experimental import pallas as pl
from jax.experimental.pallas import tpu as pltpu
from jax.sharding import Mesh
from jax.sharding import PartitionSpec as P

Z, X, Y, C = 8, 4, 4, 2
AXES = ("z", "x", "y", "c")
ROWS = ("z", "x")
COLS = ("y", "c")
PLANE = ("x", "y", "c")
TRAITS = 16
OWN = 64
CHUNKS = 8
HALF = 64
VMEM = pl.BlockSpec(memory_space=pltpu.VMEM)
SMALL = pltpu.CompilerParams(vmem_limit_bytes=2 << 20)
LARGE = pltpu.CompilerParams(vmem_limit_bytes=16 << 20)
WHOLE = pltpu.CompilerParams(vmem_limit_bytes=48 << 20)


def number(z, x, y, c):
    return ((z * X + x) * Y + y) * C + c


SENDER = (
    (7, 1, 5, 3, 0, 2, 6, 4),
    (4, 2, 5, 3, 6, 1, 0, 7),
    (6, 7, 0, 1, 5, 3, 4, 2),
    (0, 5, 7, 4, 6, 1, 2, 3),
    (0, 4, 2, 1, 3, 7, 6, 5),
    (1, 7, 5, 3, 4, 0, 2, 6),
    (7, 2, 4, 1, 3, 6, 0, 5),
    (2, 4, 1, 6, 7, 5, 3, 0),
)


def plane_to_column():
    return [
        (number(p, x, *divmod(SENDER[p][z], C)), number(z, x, *divmod(p, C))) for p in range(Z) for x in range(X) for z in range(Z)
    ]


def low_lanes(shape):
    return lax.broadcasted_iota(jnp.int32, shape, len(shape) - 1) < HALF


def unpacked(a, b):
    low = low_lanes(a.shape)
    top = jnp.where(low, a, pltpu.roll(b, HALF, 1))
    bottom = jnp.where(low, pltpu.roll(a, HALF, 1), b)
    return jnp.concatenate([top, bottom], axis=0)


def packed(tile):
    top, bottom = tile[:8], tile[8:]
    low = low_lanes(top.shape)
    return jnp.where(low, top, pltpu.roll(bottom, HALF, 1)), jnp.where(low, pltpu.roll(top, HALF, 1), bottom)


def split(x):
    high = x.astype(jnp.bfloat16)
    return high, (x - high.astype(jnp.float32)).astype(jnp.bfloat16)


def nt(left, right):
    return lax.dot_general(left, right, (((1,), (1,)), ((), ())), preferred_element_type=jnp.float32)


def nn(left, right):
    return lax.dot_general(left, right, (((1,), (0,)), ((), ())), preferred_element_type=jnp.float32)


def pack_kernel(panel_ref, out_ref):
    panel = panel_ref[...]
    piece = jnp.concatenate([panel[:8], panel[8:]], axis=1)
    out_ref[...] = jnp.broadcast_to(piece[None], out_ref.shape)


def prepare_kernel(slab_ref, kinship_ref, high_ref, low_ref, buffer, sems):
    rows = kinship_ref.shape[0]
    height = rows // CHUNKS

    def copy(i):
        return pltpu.make_async_copy(kinship_ref.at[pl.ds(i * height, height)], buffer.at[i], sems.at[i])

    for i in range(CHUNKS):
        copy(i).start()
    start = lax.axis_index("x") * (Y * C)
    own = jnp.concatenate([unpacked(slab_ref[start + j], slab_ref[start + j + 1]) for j in range(0, Y * C, 2)], axis=1)
    own = jnp.concatenate(split(own), axis=0)
    for i in range(CHUNKS):
        copy(i).wait()
        high, low = split(buffer[i])
        high_ref[pl.ds(i * height, height), :] = high
        low_ref[pl.ds(i * height, height), :] = low
    form = nn(own, high_ref[:rows, :]) + nn(own, low_ref[:rows, :])
    high, low = split(form[:TRAITS] + form[TRAITS:])
    high_ref[rows:, :] = jnp.concatenate([high] * 4 + [low] * 4, axis=0)


def half_product(block_ref, high_ref, low_ref, start):
    columns = block_ref.shape[0] * OWN
    tiles = [unpacked(block_ref[j], block_ref[j + 1]) for j in range(0, block_ref.shape[0], 2)]
    panel = jnp.concatenate(split(jnp.concatenate(tiles, axis=1)), axis=0)
    rows = low_ref.shape[0]
    both = nt(panel, high_ref[:, start : start + columns])
    partial = both[:, :rows] + nt(panel, low_ref[:, start : start + columns])
    return partial[:TRAITS] + partial[TRAITS:], both[:TRAITS, rows:] + both[TRAITS:, rows:]


def first_kernel(block_ref, high_ref, low_ref, partial_ref, wide_ref):
    partial_ref[...], wide_ref[...] = half_product(block_ref, high_ref, low_ref, 0)


def second_kernel(block_ref, high_ref, low_ref, partial_ref, wide_ref, out_ref):
    total, wide = half_product(block_ref, high_ref, low_ref, block_ref.shape[0] * OWN)
    total = total + partial_ref[...]
    wide = wide + wide_ref[...]
    wide = wide + pltpu.roll(wide, HALF, 1)
    row = lax.broadcasted_iota(jnp.int32, wide.shape, 0) % 8
    lane = lax.broadcasted_iota(jnp.int32, wide.shape, 1) // TRAITS
    wide = jnp.where(row == lane, wide, 0.0)
    top = jnp.sum(wide[:8], axis=0, keepdims=True)
    bottom = jnp.sum(wide[8:], axis=0, keepdims=True)
    score = jnp.concatenate([top, bottom, jnp.zeros((6, 128), jnp.float32)], axis=0)
    for y in range(Y):
        pair = packed(total[:, y * 128 : (y + 1) * 128])
        for c in range(C):
            out_ref[y * C + c, :8, :] = pair[c]
            out_ref[y * C + c, 8:, :] = score


def own_kernel(parts_ref, own_ref, score_ref):
    total = jnp.sum(parts_ref[...], axis=0)
    own_ref[...] = total[:8]
    score_ref[...] = jnp.broadcast_to(total[8:10][None], score_ref.shape)


def result_kernel(own_ref, parts_ref, kin_ref, score_ref, *, scale):
    own = own_ref[...]
    kin_ref[:8, :] = own[:, :HALF]
    kin_ref[8:, :] = pltpu.roll(own, HALF, 1)[:, :HALF]
    total = jnp.sum(parts_ref[...], axis=0)
    rows = [total[b // 8 : b // 8 + 1, b % 8 * TRAITS : (b % 8 + 1) * TRAITS] for b in range(TRAITS)]
    score_ref[...] = jnp.concatenate(rows, axis=0).T * scale


def shards(panel_t, kinship):
    f32 = jnp.float32
    slab_rows = kinship.shape[0]
    peers = X * Y * C
    pieces = pl.pallas_call(pack_kernel, out_shape=jax.ShapeDtypeStruct((peers, 8, 128), f32), in_specs=[VMEM], out_specs=VMEM, compiler_params=SMALL, name="pack")(panel_t)
    slab = lax.all_to_all(pieces, PLANE, 0, 0, tiled=True)
    pairs = plane_to_column()
    early = lax.ppermute(slab[: peers // 2], AXES, pairs)
    late = lax.ppermute(slab[peers // 2 :], AXES, pairs)
    high, low = pl.pallas_call(
        prepare_kernel,
        out_shape=(
            jax.ShapeDtypeStruct((slab_rows + 8 * TRAITS, kinship.shape[1]), jnp.bfloat16),
            jax.ShapeDtypeStruct(kinship.shape, jnp.bfloat16),
        ),
        in_specs=[VMEM, pl.BlockSpec(memory_space=pltpu.HBM)],
        out_specs=(VMEM, VMEM),
        scratch_shapes=[pltpu.VMEM((CHUNKS, slab_rows // CHUNKS, kinship.shape[1]), f32), pltpu.SemaphoreType.DMA((CHUNKS,))],
        compiler_params=WHOLE,
        name="prepare",
    )(slab, kinship)
    partial, wide = pl.pallas_call(
        first_kernel,
        out_shape=(jax.ShapeDtypeStruct((TRAITS, slab_rows), f32), jax.ShapeDtypeStruct((TRAITS, 8 * TRAITS), f32)),
        in_specs=[VMEM, VMEM, VMEM],
        out_specs=(VMEM, VMEM),
        compiler_params=LARGE,
        name="first",
    )(early, high, low)
    parts = pl.pallas_call(
        second_kernel,
        out_shape=jax.ShapeDtypeStruct((Y * C, 16, 128), f32),
        in_specs=[VMEM] * 5,
        out_specs=VMEM,
        compiler_params=LARGE,
        name="second",
    )(late, high, low, partial, wide)
    parts = lax.all_to_all(parts, COLS, 0, 0, tiled=True)
    own, scores = pl.pallas_call(
        own_kernel,
        out_shape=(jax.ShapeDtypeStruct((8, 128), f32), jax.ShapeDtypeStruct((Z * X, 2, 128), f32)),
        in_specs=[VMEM],
        out_specs=(VMEM, VMEM),
        compiler_params=SMALL,
        name="own",
    )(parts)
    scores = lax.all_to_all(scores, ROWS, 0, 0, tiled=True)
    samples = OWN * Z * X * Y * C
    return pl.pallas_call(
        lambda *refs: result_kernel(*refs, scale=samples**-0.5),
        out_shape=(jax.ShapeDtypeStruct(panel_t.shape, f32), jax.ShapeDtypeStruct((TRAITS, TRAITS), f32)),
        in_specs=[VMEM, VMEM],
        out_specs=(VMEM, VMEM),
        compiler_params=SMALL,
        name="result",
    )(own, scores)


def solution(mesh):
    torus = Mesh(mesh.devices.reshape(Z, X, Y, C), AXES)
    return jax.shard_map(
        shards,
        mesh=torus,
        in_specs=(P(None, AXES), P(ROWS, COLS)),
        out_specs=(P(None, AXES), P()),
        check_vma=False,
    )
```

```python
import jax
import jax.numpy as jnp
from jax import lax
from jax.experimental import pallas as pl
from jax.experimental.pallas import tpu as pltpu
from jax.sharding import Mesh
from jax.sharding import PartitionSpec as P

Z, X, Y, C = 8, 4, 4, 2
AXES = ("z", "x", "y", "c")
ROWS = ("z", "x")
COLS = ("y", "c")
PLANE = ("x", "y", "c")
TRAITS = 16
OWN = 64
CHUNKS = 8
HALF = 64
VMEM = pl.BlockSpec(memory_space=pltpu.VMEM)
SMALL = pltpu.CompilerParams(vmem_limit_bytes=2 << 20)
LARGE = pltpu.CompilerParams(vmem_limit_bytes=16 << 20)
WHOLE = pltpu.CompilerParams(vmem_limit_bytes=48 << 20)


def number(z, x, y, c):
    return ((z * X + x) * Y + y) * C + c


SENDER = (
    (7, 1, 5, 3, 0, 2, 6, 4),
    (4, 2, 5, 3, 6, 1, 0, 7),
    (6, 7, 0, 1, 5, 3, 4, 2),
    (0, 5, 7, 4, 6, 1, 2, 3),
    (0, 4, 2, 1, 3, 7, 6, 5),
    (1, 7, 5, 3, 4, 0, 2, 6),
    (7, 2, 4, 1, 3, 6, 0, 5),
    (2, 4, 1, 6, 7, 5, 3, 0),
)


def plane_to_column():
    return [
        (number(p, x, *divmod(SENDER[p][z], C)), number(z, x, *divmod(p, C))) for p in range(Z) for x in range(X) for z in range(Z)
    ]


def low_lanes(shape):
    return lax.broadcasted_iota(jnp.int32, shape, len(shape) - 1) < HALF


def unpacked(a, b):
    low = low_lanes(a.shape)
    top = jnp.where(low, a, pltpu.roll(b, HALF, 1))
    bottom = jnp.where(low, pltpu.roll(a, HALF, 1), b)
    return jnp.concatenate([top, bottom], axis=0)


def packed(tile):
    top, bottom = tile[:8], tile[8:]
    low = low_lanes(top.shape)
    return jnp.where(low, top, pltpu.roll(bottom, HALF, 1)), jnp.where(low, pltpu.roll(top, HALF, 1), bottom)


def split(x):
    high = x.astype(jnp.bfloat16)
    return high, (x - high.astype(jnp.float32)).astype(jnp.bfloat16)


def nt(left, right):
    return lax.dot_general(left, right, (((1,), (1,)), ((), ())), preferred_element_type=jnp.float32)


def nn(left, right):
    return lax.dot_general(left, right, (((1,), (0,)), ((), ())), preferred_element_type=jnp.float32)


def pack_kernel(panel_ref, out_ref):
    panel = panel_ref[...]
    piece = jnp.concatenate([panel[:8], panel[8:]], axis=1)
    out_ref[...] = jnp.broadcast_to(piece[None], out_ref.shape)


def prepare_kernel(slab_ref, kinship_ref, high_ref, low_ref, buffer, sems):
    rows = kinship_ref.shape[0]
    height = rows // CHUNKS

    def copy(i):
        return pltpu.make_async_copy(kinship_ref.at[pl.ds(i * height, height)], buffer.at[i], sems.at[i])

    for i in range(CHUNKS):
        copy(i).start()
    start = lax.axis_index("x") * (Y * C)
    own = jnp.concatenate([unpacked(slab_ref[start + j], slab_ref[start + j + 1]) for j in range(0, Y * C, 2)], axis=1)
    own = jnp.concatenate(split(own), axis=0)
    for i in range(CHUNKS):
        copy(i).wait()
        high, low = split(buffer[i])
        high_ref[pl.ds(i * height, height), :] = high
        low_ref[pl.ds(i * height, height), :] = low
    form = nn(own, high_ref[:rows, :]) + nn(own, low_ref[:rows, :])
    high, low = split(form[:TRAITS] + form[TRAITS:])
    high_ref[rows:, :] = jnp.concatenate([high] * 4 + [low] * 4, axis=0)


def product_kernel(block_ref, high_ref, low_ref, out_ref):
    columns = high_ref.shape[1]
    tiles = [unpacked(block_ref[j], block_ref[j + 1]) for j in range(0, columns // OWN, 2)]
    panel = jnp.concatenate(split(jnp.concatenate(tiles, axis=1)), axis=0)
    rows = low_ref.shape[0]
    first = nt(panel, high_ref[...])
    total = first[:, :rows] + nt(panel, low_ref[...])
    total = total[:TRAITS] + total[TRAITS:]
    wide = first[:TRAITS, rows:] + first[TRAITS:, rows:]
    wide = wide + pltpu.roll(wide, HALF, 1)
    row = lax.broadcasted_iota(jnp.int32, wide.shape, 0) % 8
    lane = lax.broadcasted_iota(jnp.int32, wide.shape, 1) // TRAITS
    wide = jnp.where(row == lane, wide, 0.0)
    top = jnp.sum(wide[:8], axis=0, keepdims=True)
    bottom = jnp.sum(wide[8:], axis=0, keepdims=True)
    score = jnp.concatenate([top, bottom, jnp.zeros((6, 128), jnp.float32)], axis=0)
    for y in range(Y):
        pair = packed(total[:, y * 128 : (y + 1) * 128])
        for c in range(C):
            out_ref[y * C + c, :8, :] = pair[c]
            out_ref[y * C + c, 8:, :] = score


def own_kernel(parts_ref, own_ref, score_ref):
    total = jnp.sum(parts_ref[...], axis=0)
    own_ref[...] = total[:8]
    score_ref[...] = jnp.broadcast_to(total[8:10][None], score_ref.shape)


def result_kernel(own_ref, parts_ref, kin_ref, score_ref, *, scale):
    own = own_ref[...]
    kin_ref[:8, :] = own[:, :HALF]
    kin_ref[8:, :] = pltpu.roll(own, HALF, 1)[:, :HALF]
    total = jnp.sum(parts_ref[...], axis=0)
    rows = [total[b // 8 : b // 8 + 1, b % 8 * TRAITS : (b % 8 + 1) * TRAITS] for b in range(TRAITS)]
    score_ref[...] = jnp.concatenate(rows, axis=0).T * scale


def shards(panel_t, kinship):
    f32 = jnp.float32
    slab_rows = kinship.shape[0]
    peers = X * Y * C
    pieces = pl.pallas_call(pack_kernel, out_shape=jax.ShapeDtypeStruct((peers, 8, 128), f32), in_specs=[VMEM], out_specs=VMEM, compiler_params=SMALL, name="pack")(panel_t)
    slab = lax.all_to_all(pieces, PLANE, 0, 0, tiled=True)
    block = lax.ppermute(slab, AXES, plane_to_column())
    high, low = pl.pallas_call(
        prepare_kernel,
        out_shape=(
            jax.ShapeDtypeStruct((slab_rows + 8 * TRAITS, kinship.shape[1]), jnp.bfloat16),
            jax.ShapeDtypeStruct(kinship.shape, jnp.bfloat16),
        ),
        in_specs=[VMEM, pl.BlockSpec(memory_space=pltpu.HBM)],
        out_specs=(VMEM, VMEM),
        scratch_shapes=[pltpu.VMEM((CHUNKS, slab_rows // CHUNKS, kinship.shape[1]), f32), pltpu.SemaphoreType.DMA((CHUNKS,))],
        compiler_params=WHOLE,
        name="prepare",
    )(slab, kinship)
    parts = pl.pallas_call(
        product_kernel,
        out_shape=jax.ShapeDtypeStruct((Y * C, 16, 128), f32),
        in_specs=[VMEM, VMEM, VMEM],
        out_specs=VMEM,
        compiler_params=LARGE,
        name="product",
    )(block, high, low)
    parts = lax.all_to_all(parts, COLS, 0, 0, tiled=True)
    own, scores = pl.pallas_call(
        own_kernel,
        out_shape=(jax.ShapeDtypeStruct((8, 128), f32), jax.ShapeDtypeStruct((Z * X, 2, 128), f32)),
        in_specs=[VMEM],
        out_specs=(VMEM, VMEM),
        compiler_params=SMALL,
        name="own",
    )(parts)
    scores = lax.all_to_all(scores, ROWS, 0, 0, tiled=True)
    samples = OWN * Z * X * Y * C
    return pl.pallas_call(
        lambda *refs: result_kernel(*refs, scale=samples**-0.5),
        out_shape=(jax.ShapeDtypeStruct(panel_t.shape, f32), jax.ShapeDtypeStruct((TRAITS, TRAITS), f32)),
        in_specs=[VMEM, VMEM],
        out_specs=(VMEM, VMEM),
        compiler_params=SMALL,
        name="result",
    )(own, scores)


def solution(mesh):
    torus = Mesh(mesh.devices.reshape(Z, X, Y, C), AXES)
    return jax.shard_map(
        shards,
        mesh=torus,
        in_specs=(P(None, AXES), P(ROWS, COLS)),
        out_specs=(P(None, AXES), P()),
        check_vma=False,
    )
```

```python
import itertools

import jax
import jax.numpy as jnp
from jax import lax
from jax.experimental import pallas as pl
from jax.experimental.pallas import tpu as pltpu
from jax.sharding import Mesh
from jax.sharding import PartitionSpec as P

Z, X, Y, C = 8, 4, 4, 2
AXES = ("z", "x", "y", "c")
ROWS = ("z", "x")
COLS = ("y", "c")
PLANE = ("x", "y", "c")
TRAITS = 16
OWN = 64
PARTS = 2
CHUNKS = 8
HALF = 64
VMEM = pl.BlockSpec(memory_space=pltpu.VMEM)
SMALL = pltpu.CompilerParams(vmem_limit_bytes=2 << 20)
LARGE = pltpu.CompilerParams(vmem_limit_bytes=16 << 20)
WHOLE = pltpu.CompilerParams(vmem_limit_bytes=48 << 20)


def number(z, x, y, c):
    return ((z * X + x) * Y + y) * C + c


def apart(a, b, n):
    d = abs(a - b) % n
    return min(d, n - d)


def plane_to_column():
    pairs = []
    for plane in range(Z):
        y_to, c_to = divmod(plane, C)
        senders = sorted(itertools.product(range(Y), range(C)), key=lambda s: (-apart(s[0], y_to, Y), (s[0] - y_to) % Y, s[1] != c_to))
        planes = sorted(range(Z), key=lambda z: (apart(z, plane, Z), (z - plane) % Z))
        for x in range(X):
            for (y, c), z in zip(senders, planes):
                pairs.append((number(plane, x, y, c), number(z, x, y_to, c_to)))
    return pairs


def low_lanes(shape):
    return lax.broadcasted_iota(jnp.int32, shape, len(shape) - 1) < HALF


def unpacked(a, b):
    low = low_lanes(a.shape)
    top = jnp.where(low, a, pltpu.roll(b, HALF, 1))
    bottom = jnp.where(low, pltpu.roll(a, HALF, 1), b)
    return jnp.concatenate([top, bottom], axis=0)


def packed(tile):
    top, bottom = tile[:8], tile[8:]
    low = low_lanes(top.shape)
    return jnp.where(low, top, pltpu.roll(bottom, HALF, 1)), jnp.where(low, pltpu.roll(top, HALF, 1), bottom)


def split(x):
    high = x.astype(jnp.bfloat16)
    return high, (x - high.astype(jnp.float32)).astype(jnp.bfloat16)


def nt(left, right):
    return lax.dot_general(left, right, (((1,), (1,)), ((), ())), preferred_element_type=jnp.float32)


def nn(left, right):
    return lax.dot_general(left, right, (((1,), (0,)), ((), ())), preferred_element_type=jnp.float32)


def pack_kernel(panel_ref, out_ref):
    panel = panel_ref[...]
    piece = jnp.concatenate([panel[:8], panel[8:]], axis=1)
    out_ref[...] = jnp.broadcast_to(piece[None], out_ref.shape)


def prepare_kernel(slab_ref, kinship_ref, high_ref, low_ref, buffer, sems):
    rows = kinship_ref.shape[0]
    height = rows // CHUNKS

    def copy(i):
        return pltpu.make_async_copy(kinship_ref.at[pl.ds(i * height, height)], buffer.at[i], sems.at[i])

    for i in range(CHUNKS):
        copy(i).start()
    start = lax.axis_index("x") * (Y * C)
    own = jnp.concatenate([unpacked(slab_ref[start + j], slab_ref[start + j + 1]) for j in range(0, Y * C, 2)], axis=1)
    own = jnp.concatenate(split(own), axis=0)
    for i in range(CHUNKS):
        copy(i).wait()
        high, low = split(buffer[i])
        high_ref[pl.ds(i * height, height), :] = high
        low_ref[pl.ds(i * height, height), :] = low
    form = nn(own, high_ref[:rows, :]) + nn(own, low_ref[:rows, :])
    high, low = split(form[:TRAITS] + form[TRAITS:])
    high_ref[rows:, :] = jnp.concatenate([high] * 4 + [low] * 4, axis=0)


def product_kernel(*refs):
    *blocks, high_ref, low_ref, out_ref = refs
    tiles = [unpacked(block[j], block[j + 1]) for block in blocks for j in range(0, block.shape[0], 2)]
    panel = jnp.concatenate(split(jnp.concatenate(tiles, axis=1)), axis=0)
    rows = low_ref.shape[0]
    first = nt(panel, high_ref[...])
    total = first[:, :rows] + nt(panel, low_ref[...])
    total = total[:TRAITS] + total[TRAITS:]
    wide = first[:TRAITS, rows:] + first[TRAITS:, rows:]
    wide = wide + pltpu.roll(wide, HALF, 1)
    row = lax.broadcasted_iota(jnp.int32, wide.shape, 0) % 8
    lane = lax.broadcasted_iota(jnp.int32, wide.shape, 1) // TRAITS
    wide = jnp.where(row == lane, wide, 0.0)
    top = jnp.sum(wide[:8], axis=0, keepdims=True)
    bottom = jnp.sum(wide[8:], axis=0, keepdims=True)
    score = jnp.concatenate([top, bottom, jnp.zeros((6, 128), jnp.float32)], axis=0)
    for y in range(Y):
        pair = packed(total[:, y * 128 : (y + 1) * 128])
        for c in range(C):
            out_ref[y * C + c, :8, :] = pair[c]
            out_ref[y * C + c, 8:, :] = score


def own_kernel(parts_ref, own_ref, score_ref):
    total = jnp.sum(parts_ref[...], axis=0)
    own_ref[...] = total[:8]
    score_ref[...] = jnp.broadcast_to(total[8:10][None], score_ref.shape)


def result_kernel(own_ref, parts_ref, kin_ref, score_ref, *, scale):
    own = own_ref[...]
    kin_ref[:8, :] = own[:, :HALF]
    kin_ref[8:, :] = pltpu.roll(own, HALF, 1)[:, :HALF]
    total = jnp.sum(parts_ref[...], axis=0)
    rows = [total[b // 8 : b // 8 + 1, b % 8 * TRAITS : (b % 8 + 1) * TRAITS] for b in range(TRAITS)]
    score_ref[...] = jnp.concatenate(rows, axis=0).T * scale


def shards(panel_t, kinship):
    f32 = jnp.float32
    slab_rows = kinship.shape[0]
    peers = X * Y * C
    pieces = pl.pallas_call(pack_kernel, out_shape=jax.ShapeDtypeStruct((peers, 8, 128), f32), in_specs=[VMEM], out_specs=VMEM, compiler_params=SMALL, name="pack")(panel_t)
    slab = lax.all_to_all(pieces, PLANE, 0, 0, tiled=True)
    pairs = plane_to_column()
    blocks = [lax.ppermute(part, AXES, pairs) for part in jnp.split(slab, PARTS)]
    high, low = pl.pallas_call(
        prepare_kernel,
        out_shape=(
            jax.ShapeDtypeStruct((slab_rows + 8 * TRAITS, kinship.shape[1]), jnp.bfloat16),
            jax.ShapeDtypeStruct(kinship.shape, jnp.bfloat16),
        ),
        in_specs=[VMEM, pl.BlockSpec(memory_space=pltpu.HBM)],
        out_specs=(VMEM, VMEM),
        scratch_shapes=[pltpu.VMEM((CHUNKS, slab_rows // CHUNKS, kinship.shape[1]), f32), pltpu.SemaphoreType.DMA((CHUNKS,))],
        compiler_params=WHOLE,
        name="prepare",
    )(slab, kinship)
    parts = pl.pallas_call(
        product_kernel,
        out_shape=jax.ShapeDtypeStruct((Y * C, 16, 128), f32),
        in_specs=[VMEM] * (PARTS + 2),
        out_specs=VMEM,
        compiler_params=LARGE,
        name="product",
    )(*blocks, high, low)
    parts = lax.all_to_all(parts, COLS, 0, 0, tiled=True)
    own, scores = pl.pallas_call(
        own_kernel,
        out_shape=(jax.ShapeDtypeStruct((8, 128), f32), jax.ShapeDtypeStruct((Z * X, 2, 128), f32)),
        in_specs=[VMEM],
        out_specs=(VMEM, VMEM),
        compiler_params=SMALL,
        name="own",
    )(parts)
    scores = lax.all_to_all(scores, ROWS, 0, 0, tiled=True)
    samples = OWN * Z * X * Y * C
    return pl.pallas_call(
        lambda *refs: result_kernel(*refs, scale=samples**-0.5),
        out_shape=(jax.ShapeDtypeStruct(panel_t.shape, f32), jax.ShapeDtypeStruct((TRAITS, TRAITS), f32)),
        in_specs=[VMEM, VMEM],
        out_specs=(VMEM, VMEM),
        compiler_params=SMALL,
        name="result",
    )(own, scores)


def solution(mesh):
    torus = Mesh(mesh.devices.reshape(Z, X, Y, C), AXES)
    return jax.shard_map(
        shards,
        mesh=torus,
        in_specs=(P(None, AXES), P(ROWS, COLS)),
        out_specs=(P(None, AXES), P()),
        check_vma=False,
    )
```

```python
import itertools

import jax
import jax.numpy as jnp
from jax import lax
from jax.experimental import pallas as pl
from jax.experimental.pallas import tpu as pltpu
from jax.sharding import Mesh
from jax.sharding import PartitionSpec as P

Z, X, Y, C = 8, 4, 4, 2
AXES = ("z", "x", "y", "c")
ROWS = ("z", "x")
COLS = ("y", "c")
PLANE = ("x", "y", "c")
TRAITS = 16
OWN = 64
CHUNKS = 8
HALF = 64
VMEM = pl.BlockSpec(memory_space=pltpu.VMEM)
SMALL = pltpu.CompilerParams(vmem_limit_bytes=2 << 20)
LARGE = pltpu.CompilerParams(vmem_limit_bytes=16 << 20)
WHOLE = pltpu.CompilerParams(vmem_limit_bytes=48 << 20)


def number(z, x, y, c):
    return ((z * X + x) * Y + y) * C + c


def apart(a, b, n):
    d = abs(a - b) % n
    return min(d, n - d)


def plane_to_column():
    pairs = []
    for plane in range(Z):
        y_to, c_to = divmod(plane, C)
        senders = sorted(itertools.product(range(Y), range(C)), key=lambda s: (-apart(s[0], y_to, Y), (s[0] - y_to) % Y, s[1] != c_to))
        planes = sorted(range(Z), key=lambda z: (apart(z, plane, Z), (z - plane) % Z))
        for x in range(X):
            for (y, c), z in zip(senders, planes):
                pairs.append((number(plane, x, y, c), number(z, x, y_to, c_to)))
    return pairs


def low_lanes(shape):
    return lax.broadcasted_iota(jnp.int32, shape, len(shape) - 1) < HALF


def unpacked(a, b):
    low = low_lanes(a.shape)
    top = jnp.where(low, a, pltpu.roll(b, HALF, 1))
    bottom = jnp.where(low, pltpu.roll(a, HALF, 1), b)
    return jnp.concatenate([top, bottom], axis=0)


def packed(tile):
    top, bottom = tile[:8], tile[8:]
    low = low_lanes(top.shape)
    return jnp.where(low, top, pltpu.roll(bottom, HALF, 1)), jnp.where(low, pltpu.roll(top, HALF, 1), bottom)


def split(x):
    high = x.astype(jnp.bfloat16)
    return high, (x - high.astype(jnp.float32)).astype(jnp.bfloat16)


def nt(left, right):
    return lax.dot_general(left, right, (((1,), (1,)), ((), ())), preferred_element_type=jnp.float32)


def nn(left, right):
    return lax.dot_general(left, right, (((1,), (0,)), ((), ())), preferred_element_type=jnp.float32)


def pack_kernel(panel_ref, out_ref):
    panel = panel_ref[...]
    piece = jnp.concatenate([panel[:8], panel[8:]], axis=1)
    out_ref[...] = jnp.broadcast_to(piece[None], out_ref.shape)


def prepare_kernel(slab_ref, kinship_ref, high_ref, low_ref, buffer, sems):
    rows = kinship_ref.shape[0]
    height = rows // CHUNKS

    def copy(i):
        return pltpu.make_async_copy(kinship_ref.at[pl.ds(i * height, height)], buffer.at[i], sems.at[i])

    for i in range(CHUNKS):
        copy(i).start()
    start = lax.axis_index("x") * (Y * C)
    own = jnp.concatenate([unpacked(slab_ref[start + j], slab_ref[start + j + 1]) for j in range(0, Y * C, 2)], axis=1)
    own = jnp.concatenate(split(own), axis=0)
    for i in range(CHUNKS):
        copy(i).wait()
        high, low = split(buffer[i])
        high_ref[pl.ds(i * height, height), :] = high
        low_ref[pl.ds(i * height, height), :] = low
    form = nn(own, high_ref[:rows, :]) + nn(own, low_ref[:rows, :])
    high, low = split(form[:TRAITS] + form[TRAITS:])
    high_ref[rows:, :] = jnp.concatenate([high] * 4 + [low] * 4, axis=0)


def half_product(block_ref, high_ref, low_ref, start):
    columns = block_ref.shape[0] * OWN
    tiles = [unpacked(block_ref[j], block_ref[j + 1]) for j in range(0, block_ref.shape[0], 2)]
    panel = jnp.concatenate(split(jnp.concatenate(tiles, axis=1)), axis=0)
    rows = low_ref.shape[0]
    both = nt(panel, high_ref[:, start : start + columns])
    partial = both[:, :rows] + nt(panel, low_ref[:, start : start + columns])
    return partial[:TRAITS] + partial[TRAITS:], both[:TRAITS, rows:] + both[TRAITS:, rows:]


def first_kernel(block_ref, high_ref, low_ref, partial_ref, wide_ref):
    partial_ref[...], wide_ref[...] = half_product(block_ref, high_ref, low_ref, 0)


def second_kernel(block_ref, high_ref, low_ref, partial_ref, wide_ref, out_ref):
    total, wide = half_product(block_ref, high_ref, low_ref, block_ref.shape[0] * OWN)
    total = total + partial_ref[...]
    wide = wide + wide_ref[...]
    wide = wide + pltpu.roll(wide, HALF, 1)
    row = lax.broadcasted_iota(jnp.int32, wide.shape, 0) % 8
    lane = lax.broadcasted_iota(jnp.int32, wide.shape, 1) // TRAITS
    wide = jnp.where(row == lane, wide, 0.0)
    top = jnp.sum(wide[:8], axis=0, keepdims=True)
    bottom = jnp.sum(wide[8:], axis=0, keepdims=True)
    score = jnp.concatenate([top, bottom], axis=0)
    for y in range(Y):
        pair = packed(total[:, y * 128 : (y + 1) * 128])
        for c in range(C):
            for i in range(4):
                out_ref[y * C + c, i] = pair[c][2 * i : 2 * i + 2]
            out_ref[y * C + c, 4] = score


def own_kernel(parts_ref, own_ref, score_ref):
    total = jnp.sum(parts_ref[...], axis=0)
    for i in range(4):
        own_ref[2 * i : 2 * i + 2, :] = total[i]
    score_ref[...] = jnp.broadcast_to(total[4:], score_ref.shape)


def result_kernel(own_ref, parts_ref, kin_ref, score_ref, *, scale):
    own = own_ref[...]
    kin_ref[:8, :] = own[:, :HALF]
    kin_ref[8:, :] = pltpu.roll(own, HALF, 1)[:, :HALF]
    total = jnp.sum(parts_ref[...], axis=0)
    rows = [total[b // 8 : b // 8 + 1, b % 8 * TRAITS : (b % 8 + 1) * TRAITS] for b in range(TRAITS)]
    score_ref[...] = jnp.concatenate(rows, axis=0).T * scale


def shards(panel_t, kinship):
    f32 = jnp.float32
    slab_rows = kinship.shape[0]
    peers = X * Y * C
    pieces = pl.pallas_call(pack_kernel, out_shape=jax.ShapeDtypeStruct((peers, 8, 128), f32), in_specs=[VMEM], out_specs=VMEM, compiler_params=SMALL, name="pack")(panel_t)
    slab = lax.all_to_all(pieces, PLANE, 0, 0, tiled=True)
    pairs = plane_to_column()
    early = lax.ppermute(slab[: peers // 2], AXES, pairs)
    late = lax.ppermute(slab[peers // 2 :], AXES, pairs)
    high, low = pl.pallas_call(
        prepare_kernel,
        out_shape=(
            jax.ShapeDtypeStruct((slab_rows + 8 * TRAITS, kinship.shape[1]), jnp.bfloat16),
            jax.ShapeDtypeStruct(kinship.shape, jnp.bfloat16),
        ),
        in_specs=[VMEM, pl.BlockSpec(memory_space=pltpu.HBM)],
        out_specs=(VMEM, VMEM),
        scratch_shapes=[pltpu.VMEM((CHUNKS, slab_rows // CHUNKS, kinship.shape[1]), f32), pltpu.SemaphoreType.DMA((CHUNKS,))],
        compiler_params=WHOLE,
        name="prepare",
    )(slab, kinship)
    partial, wide = pl.pallas_call(
        first_kernel,
        out_shape=(jax.ShapeDtypeStruct((TRAITS, slab_rows), f32), jax.ShapeDtypeStruct((TRAITS, 8 * TRAITS), f32)),
        in_specs=[VMEM, VMEM, VMEM],
        out_specs=(VMEM, VMEM),
        compiler_params=LARGE,
        name="first",
    )(early, high, low)
    parts = pl.pallas_call(
        second_kernel,
        out_shape=jax.ShapeDtypeStruct((Y * C, 5, 2, 128), f32),
        in_specs=[VMEM] * 5,
        out_specs=VMEM,
        compiler_params=LARGE,
        name="second",
    )(late, high, low, partial, wide)
    parts = lax.all_to_all(parts, COLS, 0, 0, tiled=True)
    own, scores = pl.pallas_call(
        own_kernel,
        out_shape=(jax.ShapeDtypeStruct((8, 128), f32), jax.ShapeDtypeStruct((Z * X, 2, 128), f32)),
        in_specs=[VMEM],
        out_specs=(VMEM, VMEM),
        compiler_params=SMALL,
        name="own",
    )(parts)
    scores = lax.all_to_all(scores, ROWS, 0, 0, tiled=True)
    samples = OWN * Z * X * Y * C
    return pl.pallas_call(
        lambda *refs: result_kernel(*refs, scale=samples**-0.5),
        out_shape=(jax.ShapeDtypeStruct(panel_t.shape, f32), jax.ShapeDtypeStruct((TRAITS, TRAITS), f32)),
        in_specs=[VMEM, VMEM],
        out_specs=(VMEM, VMEM),
        compiler_params=SMALL,
        name="result",
    )(own, scores)


def solution(mesh):
    torus = Mesh(mesh.devices.reshape(Z, X, Y, C), AXES)
    return jax.shard_map(
        shards,
        mesh=torus,
        in_specs=(P(None, AXES), P(ROWS, COLS)),
        out_specs=(P(None, AXES), P()),
        check_vma=False,
    )
```

```python
import itertools

import jax
import jax.numpy as jnp
from jax import lax
from jax.experimental import pallas as pl
from jax.experimental.pallas import tpu as pltpu
from jax.sharding import Mesh
from jax.sharding import PartitionSpec as P

Z, X, Y, C = 8, 4, 4, 2
AXES = ("z", "x", "y", "c")
ROWS = ("z", "x")
COLS = ("y", "c")
PLANE = ("x", "y", "c")
TRAITS = 16
OWN = 64
CHUNKS = 4
HALF = 64
VMEM = pl.BlockSpec(memory_space=pltpu.VMEM)
SMALL = pltpu.CompilerParams(vmem_limit_bytes=2 << 20)
LARGE = pltpu.CompilerParams(vmem_limit_bytes=16 << 20)
WHOLE = pltpu.CompilerParams(vmem_limit_bytes=48 << 20)


def number(z, x, y, c):
    return ((z * X + x) * Y + y) * C + c


def apart(a, b, n):
    d = abs(a - b) % n
    return min(d, n - d)


def plane_to_column():
    pairs = []
    for plane in range(Z):
        y_to, c_to = divmod(plane, C)
        senders = sorted(itertools.product(range(Y), range(C)), key=lambda s: (-apart(s[0], y_to, Y), (s[0] - y_to) % Y, s[1] != c_to))
        planes = sorted(range(Z), key=lambda z: (apart(z, plane, Z), (z - plane) % Z))
        for x in range(X):
            for (y, c), z in zip(senders, planes):
                pairs.append((number(plane, x, y, c), number(z, x, y_to, c_to)))
    return pairs


def low_lanes(shape):
    return lax.broadcasted_iota(jnp.int32, shape, len(shape) - 1) < HALF


def unpacked(a, b):
    low = low_lanes(a.shape)
    top = jnp.where(low, a, pltpu.roll(b, HALF, 1))
    bottom = jnp.where(low, pltpu.roll(a, HALF, 1), b)
    return jnp.concatenate([top, bottom], axis=0)


def packed(tile):
    top, bottom = tile[:8], tile[8:]
    low = low_lanes(top.shape)
    return jnp.where(low, top, pltpu.roll(bottom, HALF, 1)), jnp.where(low, pltpu.roll(top, HALF, 1), bottom)


def split(x):
    high = x.astype(jnp.bfloat16)
    return high, (x - high.astype(jnp.float32)).astype(jnp.bfloat16)


def nn(left, right):
    return lax.dot_general(left, right, (((1,), (0,)), ((), ())), preferred_element_type=jnp.float32)


def pack_kernel(panel_ref, out_ref):
    panel = panel_ref[...]
    piece = jnp.concatenate([panel[:8], panel[8:]], axis=1)
    out_ref[...] = jnp.broadcast_to(piece[None], out_ref.shape)


def prepare_kernel(slab_ref, kinship_ref, high_ref, low_ref, buffer, sems):
    rows = kinship_ref.shape[0]
    height = rows // CHUNKS

    def copy(i):
        return pltpu.make_async_copy(kinship_ref.at[pl.ds(i * height, height)], buffer.at[i], sems.at[i])

    for i in range(CHUNKS):
        copy(i).start()
    start = lax.axis_index("x") * (Y * C)
    own = jnp.concatenate([unpacked(slab_ref[start + j], slab_ref[start + j + 1]) for j in range(0, Y * C, 2)], axis=1)
    own = jnp.concatenate(split(own), axis=0)
    form = jnp.zeros((2 * TRAITS, kinship_ref.shape[1]), jnp.float32)
    for i in range(CHUNKS):
        copy(i).wait()
        across = slice(i * height, (i + 1) * height)
        high_ref[:, across], low_ref[:, across] = split(buffer[i].T)
        for part in split(buffer[i]):
            form = form + nn(own[:, across], part)
    form = form[:TRAITS] + form[TRAITS:]
    high, low = (part.astype(jnp.float32) for part in split(form))
    high_ref[:, rows:] = jnp.concatenate([high] * 4 + [low] * 4, axis=0).T.astype(jnp.bfloat16)


def half_product(block_ref, high_ref, low_ref, start):
    columns = block_ref.shape[0] * OWN
    tiles = [unpacked(block_ref[j], block_ref[j + 1]) for j in range(0, block_ref.shape[0], 2)]
    panel = jnp.concatenate(split(jnp.concatenate(tiles, axis=1)), axis=0)
    rows = low_ref.shape[1]
    both = nn(panel, high_ref[start : start + columns, :])
    partial = both[:, :rows] + nn(panel, low_ref[start : start + columns, :])
    return partial[:TRAITS] + partial[TRAITS:], both[:TRAITS, rows:] + both[TRAITS:, rows:]


def first_kernel(block_ref, high_ref, low_ref, partial_ref, wide_ref):
    partial_ref[...], wide_ref[...] = half_product(block_ref, high_ref, low_ref, 0)


def second_kernel(block_ref, high_ref, low_ref, partial_ref, wide_ref, out_ref):
    total, wide = half_product(block_ref, high_ref, low_ref, block_ref.shape[0] * OWN)
    total = total + partial_ref[...]
    wide = wide + wide_ref[...]
    wide = wide + pltpu.roll(wide, HALF, 1)
    row = lax.broadcasted_iota(jnp.int32, wide.shape, 0) % 8
    lane = lax.broadcasted_iota(jnp.int32, wide.shape, 1) // TRAITS
    wide = jnp.where(row == lane, wide, 0.0)
    top = jnp.sum(wide[:8], axis=0, keepdims=True)
    bottom = jnp.sum(wide[8:], axis=0, keepdims=True)
    score = jnp.concatenate([top, bottom], axis=0)
    for y in range(Y):
        pair = packed(total[:, y * 128 : (y + 1) * 128])
        for c in range(C):
            for i in range(4):
                out_ref[y * C + c, i] = pair[c][2 * i : 2 * i + 2]
            out_ref[y * C + c, 4] = score


def own_kernel(parts_ref, own_ref, score_ref):
    total = jnp.sum(parts_ref[...], axis=0)
    for i in range(4):
        own_ref[2 * i : 2 * i + 2, :] = total[i]
    score_ref[...] = jnp.broadcast_to(total[4:], score_ref.shape)


def result_kernel(own_ref, parts_ref, kin_ref, score_ref, *, scale):
    own = own_ref[...]
    kin_ref[:8, :] = own[:, :HALF]
    kin_ref[8:, :] = pltpu.roll(own, HALF, 1)[:, :HALF]
    total = jnp.sum(parts_ref[...], axis=0)
    rows = [total[b // 8 : b // 8 + 1, b % 8 * TRAITS : (b % 8 + 1) * TRAITS] for b in range(TRAITS)]
    score_ref[...] = jnp.concatenate(rows, axis=0).T * scale


def shards(panel_t, kinship):
    f32 = jnp.float32
    slab_rows = kinship.shape[0]
    peers = X * Y * C
    pieces = pl.pallas_call(pack_kernel, out_shape=jax.ShapeDtypeStruct((peers, 8, 128), f32), in_specs=[VMEM], out_specs=VMEM, compiler_params=SMALL, name="pack")(panel_t)
    slab = lax.all_to_all(pieces, PLANE, 0, 0, tiled=True)
    pairs = plane_to_column()
    early = lax.ppermute(slab[: peers // 2], AXES, pairs)
    late = lax.ppermute(slab[peers // 2 :], AXES, pairs)
    high, low = pl.pallas_call(
        prepare_kernel,
        out_shape=(
            jax.ShapeDtypeStruct((kinship.shape[1], slab_rows + 8 * TRAITS), jnp.bfloat16),
            jax.ShapeDtypeStruct(kinship.shape[::-1], jnp.bfloat16),
        ),
        in_specs=[VMEM, pl.BlockSpec(memory_space=pltpu.HBM)],
        out_specs=(VMEM, VMEM),
        scratch_shapes=[pltpu.VMEM((CHUNKS, slab_rows // CHUNKS, kinship.shape[1]), f32), pltpu.SemaphoreType.DMA((CHUNKS,))],
        compiler_params=WHOLE,
        name="prepare",
    )(slab, kinship)
    partial, wide = pl.pallas_call(
        first_kernel,
        out_shape=(jax.ShapeDtypeStruct((TRAITS, slab_rows), f32), jax.ShapeDtypeStruct((TRAITS, 8 * TRAITS), f32)),
        in_specs=[VMEM, VMEM, VMEM],
        out_specs=(VMEM, VMEM),
        compiler_params=LARGE,
        name="first",
    )(early, high, low)
    parts = pl.pallas_call(
        second_kernel,
        out_shape=jax.ShapeDtypeStruct((Y * C, 5, 2, 128), f32),
        in_specs=[VMEM] * 5,
        out_specs=VMEM,
        compiler_params=LARGE,
        name="second",
    )(late, high, low, partial, wide)
    parts = lax.all_to_all(parts, COLS, 0, 0, tiled=True)
    own, scores = pl.pallas_call(
        own_kernel,
        out_shape=(jax.ShapeDtypeStruct((8, 128), f32), jax.ShapeDtypeStruct((Z * X, 2, 128), f32)),
        in_specs=[VMEM],
        out_specs=(VMEM, VMEM),
        compiler_params=SMALL,
        name="own",
    )(parts)
    scores = lax.all_to_all(scores, ROWS, 0, 0, tiled=True)
    samples = OWN * Z * X * Y * C
    return pl.pallas_call(
        lambda *refs: result_kernel(*refs, scale=samples**-0.5),
        out_shape=(jax.ShapeDtypeStruct(panel_t.shape, f32), jax.ShapeDtypeStruct((TRAITS, TRAITS), f32)),
        in_specs=[VMEM, VMEM],
        out_specs=(VMEM, VMEM),
        compiler_params=SMALL,
        name="result",
    )(own, scores)


def solution(mesh):
    torus = Mesh(mesh.devices.reshape(Z, X, Y, C), AXES)
    return jax.shard_map(
        shards,
        mesh=torus,
        in_specs=(P(None, AXES), P(ROWS, COLS)),
        out_specs=(P(None, AXES), P()),
        check_vma=False,
    )
```

```python
import jax
import jax.numpy as jnp
from jax import lax
from jax.experimental import pallas as pl
from jax.experimental.pallas import tpu as pltpu
from jax.sharding import Mesh
from jax.sharding import PartitionSpec as P

Z, X, Y, C = 8, 4, 4, 2
AXES = ("z", "x", "y", "c")
ROWS = ("z", "x")
COLS = ("y", "c")
PLANE = ("x", "y", "c")
TRAITS = 16
OWN = 64
CHUNKS = 4
HALF = 64
VMEM = pl.BlockSpec(memory_space=pltpu.VMEM)
SMALL = pltpu.CompilerParams(vmem_limit_bytes=2 << 20)
LARGE = pltpu.CompilerParams(vmem_limit_bytes=16 << 20)
WHOLE = pltpu.CompilerParams(vmem_limit_bytes=48 << 20)


def number(z, x, y, c):
    return ((z * X + x) * Y + y) * C + c


SENDER = (
    (6, 2, 5, 0, 1, 3, 7, 4),
    (5, 4, 3, 2, 7, 0, 1, 6),
    (0, 6, 1, 7, 4, 2, 3, 5),
    (2, 1, 6, 5, 7, 4, 0, 3),
    (4, 7, 2, 1, 3, 0, 6, 5),
    (7, 5, 4, 2, 0, 6, 3, 1),
    (3, 0, 7, 1, 4, 2, 5, 6),
    (0, 2, 5, 6, 7, 4, 3, 1),
)


def plane_to_column():
    return [
        (number(p, x, *divmod(SENDER[p][z], C)), number(z, x, *divmod(p, C))) for p in range(Z) for x in range(X) for z in range(Z)
    ]


def low_lanes(shape):
    return lax.broadcasted_iota(jnp.int32, shape, len(shape) - 1) < HALF


def unpacked(a, b):
    low = low_lanes(a.shape)
    top = jnp.where(low, a, pltpu.roll(b, HALF, 1))
    bottom = jnp.where(low, pltpu.roll(a, HALF, 1), b)
    return jnp.concatenate([top, bottom], axis=0)


def packed(tile):
    top, bottom = tile[:8], tile[8:]
    low = low_lanes(top.shape)
    return jnp.where(low, top, pltpu.roll(bottom, HALF, 1)), jnp.where(low, pltpu.roll(top, HALF, 1), bottom)


def split(x):
    high = x.astype(jnp.bfloat16)
    return high, (x - high.astype(jnp.float32)).astype(jnp.bfloat16)


def nn(left, right):
    return lax.dot_general(left, right, (((1,), (0,)), ((), ())), preferred_element_type=jnp.float32)


def pack_kernel(panel_ref, out_ref):
    panel = panel_ref[...]
    piece = jnp.concatenate([panel[:8], panel[8:]], axis=1)
    out_ref[...] = jnp.broadcast_to(piece[None], out_ref.shape)


def prepare_kernel(slab_ref, kinship_ref, high_ref, low_ref, buffer, sems):
    rows = kinship_ref.shape[0]
    height = rows // CHUNKS

    def copy(i):
        return pltpu.make_async_copy(kinship_ref.at[pl.ds(i * height, height)], buffer.at[i], sems.at[i])

    for i in range(CHUNKS):
        copy(i).start()
    start = lax.axis_index("x") * (Y * C)
    own = jnp.concatenate([unpacked(slab_ref[start + j], slab_ref[start + j + 1]) for j in range(0, Y * C, 2)], axis=1)
    own = jnp.concatenate(split(own), axis=0)
    form = jnp.zeros((2 * TRAITS, kinship_ref.shape[1]), jnp.float32)
    for i in range(CHUNKS):
        copy(i).wait()
        across = slice(i * height, (i + 1) * height)
        high_ref[:, across], low_ref[:, across] = split(buffer[i].T)
        for part in split(buffer[i]):
            form = form + nn(own[:, across], part)
    form = form[:TRAITS] + form[TRAITS:]
    high, low = (part.astype(jnp.float32) for part in split(form))
    high_ref[:, rows:] = jnp.concatenate([high] * 4 + [low] * 4, axis=0).T.astype(jnp.bfloat16)


def half_product(block_ref, high_ref, low_ref, start):
    columns = block_ref.shape[0] * OWN
    tiles = [unpacked(block_ref[j], block_ref[j + 1]) for j in range(0, block_ref.shape[0], 2)]
    panel = jnp.concatenate(split(jnp.concatenate(tiles, axis=1)), axis=0)
    rows = low_ref.shape[1]
    both = nn(panel, high_ref[start : start + columns, :])
    partial = both[:, :rows] + nn(panel, low_ref[start : start + columns, :])
    return partial[:TRAITS] + partial[TRAITS:], both[:TRAITS, rows:] + both[TRAITS:, rows:]


def first_kernel(block_ref, high_ref, low_ref, partial_ref, wide_ref):
    partial_ref[...], wide_ref[...] = half_product(block_ref, high_ref, low_ref, 0)


def second_kernel(block_ref, high_ref, low_ref, partial_ref, wide_ref, out_ref):
    total, wide = half_product(block_ref, high_ref, low_ref, block_ref.shape[0] * OWN)
    total = total + partial_ref[...]
    wide = wide + wide_ref[...]
    wide = wide + pltpu.roll(wide, HALF, 1)
    row = lax.broadcasted_iota(jnp.int32, wide.shape, 0) % 8
    lane = lax.broadcasted_iota(jnp.int32, wide.shape, 1) // TRAITS
    wide = jnp.where(row == lane, wide, 0.0)
    top = jnp.sum(wide[:8], axis=0, keepdims=True)
    bottom = jnp.sum(wide[8:], axis=0, keepdims=True)
    score = jnp.concatenate([top, bottom], axis=0)
    for y in range(Y):
        pair = packed(total[:, y * 128 : (y + 1) * 128])
        for c in range(C):
            for i in range(4):
                out_ref[y * C + c, i] = pair[c][2 * i : 2 * i + 2]
            out_ref[y * C + c, 4] = score


def own_kernel(parts_ref, own_ref, score_ref):
    total = jnp.sum(parts_ref[...], axis=0)
    for i in range(4):
        own_ref[2 * i : 2 * i + 2, :] = total[i]
    score_ref[...] = jnp.broadcast_to(total[4:], score_ref.shape)


def result_kernel(own_ref, parts_ref, kin_ref, score_ref, *, scale):
    own = own_ref[...]
    kin_ref[:8, :] = own[:, :HALF]
    kin_ref[8:, :] = pltpu.roll(own, HALF, 1)[:, :HALF]
    total = jnp.sum(parts_ref[...], axis=0)
    rows = [total[b // 8 : b // 8 + 1, b % 8 * TRAITS : (b % 8 + 1) * TRAITS] for b in range(TRAITS)]
    score_ref[...] = jnp.concatenate(rows, axis=0).T * scale


def shards(panel_t, kinship):
    f32 = jnp.float32
    slab_rows = kinship.shape[0]
    peers = X * Y * C
    pieces = pl.pallas_call(pack_kernel, out_shape=jax.ShapeDtypeStruct((peers, 8, 128), f32), in_specs=[VMEM], out_specs=VMEM, compiler_params=SMALL, name="pack")(panel_t)
    slab = lax.all_to_all(pieces, PLANE, 0, 0, tiled=True)
    pairs = plane_to_column()
    early = lax.ppermute(slab[: peers // 2], AXES, pairs)
    late = lax.ppermute(slab[peers // 2 :], AXES, pairs)
    high, low = pl.pallas_call(
        prepare_kernel,
        out_shape=(
            jax.ShapeDtypeStruct((kinship.shape[1], slab_rows + 8 * TRAITS), jnp.bfloat16),
            jax.ShapeDtypeStruct(kinship.shape[::-1], jnp.bfloat16),
        ),
        in_specs=[VMEM, pl.BlockSpec(memory_space=pltpu.HBM)],
        out_specs=(VMEM, VMEM),
        scratch_shapes=[pltpu.VMEM((CHUNKS, slab_rows // CHUNKS, kinship.shape[1]), f32), pltpu.SemaphoreType.DMA((CHUNKS,))],
        compiler_params=WHOLE,
        name="prepare",
    )(slab, kinship)
    partial, wide = pl.pallas_call(
        first_kernel,
        out_shape=(jax.ShapeDtypeStruct((TRAITS, slab_rows), f32), jax.ShapeDtypeStruct((TRAITS, 8 * TRAITS), f32)),
        in_specs=[VMEM, VMEM, VMEM],
        out_specs=(VMEM, VMEM),
        compiler_params=LARGE,
        name="first",
    )(early, high, low)
    parts = pl.pallas_call(
        second_kernel,
        out_shape=jax.ShapeDtypeStruct((Y * C, 5, 2, 128), f32),
        in_specs=[VMEM] * 5,
        out_specs=VMEM,
        compiler_params=LARGE,
        name="second",
    )(late, high, low, partial, wide)
    parts = lax.all_to_all(parts, COLS, 0, 0, tiled=True)
    own, scores = pl.pallas_call(
        own_kernel,
        out_shape=(jax.ShapeDtypeStruct((8, 128), f32), jax.ShapeDtypeStruct((Z * X, 2, 128), f32)),
        in_specs=[VMEM],
        out_specs=(VMEM, VMEM),
        compiler_params=SMALL,
        name="own",
    )(parts)
    scores = lax.all_to_all(scores, ROWS, 0, 0, tiled=True)
    samples = OWN * Z * X * Y * C
    return pl.pallas_call(
        lambda *refs: result_kernel(*refs, scale=samples**-0.5),
        out_shape=(jax.ShapeDtypeStruct(panel_t.shape, f32), jax.ShapeDtypeStruct((TRAITS, TRAITS), f32)),
        in_specs=[VMEM, VMEM],
        out_specs=(VMEM, VMEM),
        compiler_params=SMALL,
        name="result",
    )(own, scores)


def solution(mesh):
    torus = Mesh(mesh.devices.reshape(Z, X, Y, C), AXES)
    return jax.shard_map(
        shards,
        mesh=torus,
        in_specs=(P(None, AXES), P(ROWS, COLS)),
        out_specs=(P(None, AXES), P()),
        check_vma=False,
    )
```

```python
import jax
import jax.numpy as jnp
from jax import lax
from jax.experimental import pallas as pl
from jax.experimental.pallas import tpu as pltpu
from jax.sharding import Mesh
from jax.sharding import PartitionSpec as P

Z, X, Y, C = 8, 4, 4, 2
AXES = ("z", "x", "y", "c")
ROWS = ("z", "x")
COLS = ("y", "c")
PLANE = ("x", "y", "c")
TRAITS = 16
OWN = 64
CHUNKS = 4
HALF = 64
VMEM = pl.BlockSpec(memory_space=pltpu.VMEM)
SMALL = pltpu.CompilerParams(vmem_limit_bytes=2 << 20)
LARGE = pltpu.CompilerParams(vmem_limit_bytes=16 << 20)
WHOLE = pltpu.CompilerParams(vmem_limit_bytes=48 << 20)


def number(z, x, y, c):
    return ((z * X + x) * Y + y) * C + c


SENDER = (
    (6, 2, 5, 0, 1, 3, 7, 4),
    (5, 4, 3, 2, 7, 0, 1, 6),
    (0, 6, 1, 7, 4, 2, 3, 5),
    (2, 1, 6, 5, 7, 4, 0, 3),
    (4, 7, 2, 1, 3, 0, 6, 5),
    (7, 5, 4, 2, 0, 6, 3, 1),
    (3, 0, 7, 1, 4, 2, 5, 6),
    (0, 2, 5, 6, 7, 4, 3, 1),
)


def plane_to_column():
    return [
        (number(p, x, *divmod(SENDER[p][z], C)), number(z, x, *divmod(p, C))) for p in range(Z) for x in range(X) for z in range(Z)
    ]


def low_lanes(shape):
    return lax.broadcasted_iota(jnp.int32, shape, len(shape) - 1) < HALF


def unpacked(a, b):
    low = low_lanes(a.shape)
    top = jnp.where(low, a, pltpu.roll(b, HALF, 1))
    bottom = jnp.where(low, pltpu.roll(a, HALF, 1), b)
    return jnp.concatenate([top, bottom], axis=0)


def packed(tile):
    top, bottom = tile[:8], tile[8:]
    low = low_lanes(top.shape)
    return jnp.where(low, top, pltpu.roll(bottom, HALF, 1)), jnp.where(low, pltpu.roll(top, HALF, 1), bottom)


def split(x):
    high = x.astype(jnp.bfloat16)
    return high, (x - high.astype(jnp.float32)).astype(jnp.bfloat16)


def nn(left, right):
    return lax.dot_general(left, right, (((1,), (0,)), ((), ())), preferred_element_type=jnp.float32)


def pack_kernel(panel_ref, out_ref):
    panel = panel_ref[...]
    piece = jnp.concatenate([panel[:8], panel[8:]], axis=1)
    out_ref[...] = jnp.broadcast_to(piece[None], out_ref.shape)


def prepare_kernel(slab_ref, kinship_ref, high_ref, low_ref, buffer, sems):
    rows = kinship_ref.shape[0]
    height = rows // CHUNKS

    def copy(i):
        return pltpu.make_async_copy(kinship_ref.at[pl.ds(i * height, height)], buffer.at[i], sems.at[i])

    for i in range(CHUNKS):
        copy(i).start()
    start = lax.axis_index("x") * (Y * C)
    own = jnp.concatenate([unpacked(slab_ref[start + j], slab_ref[start + j + 1]) for j in range(0, Y * C, 2)], axis=1)
    own = jnp.concatenate(split(own), axis=0)
    form = jnp.zeros((2 * TRAITS, kinship_ref.shape[1]), jnp.float32)
    for i in range(CHUNKS):
        copy(i).wait()
        across = slice(i * height, (i + 1) * height)
        high_ref[:, across], low_ref[:, across] = split(buffer[i].T)
        for part in split(buffer[i]):
            form = form + nn(own[:, across], part)
    form = form[:TRAITS] + form[TRAITS:]
    high, low = (part.astype(jnp.float32) for part in split(form))
    high_ref[:, rows:] = jnp.concatenate([high] * 4 + [low] * 4, axis=0).T.astype(jnp.bfloat16)


def product_kernel(block_ref, high_ref, low_ref, out_ref):
    tiles = [unpacked(block_ref[j], block_ref[j + 1]) for j in range(0, block_ref.shape[0], 2)]
    panel = jnp.concatenate(split(jnp.concatenate(tiles, axis=1)), axis=0)
    rows = low_ref.shape[1]
    both = nn(panel, high_ref[...])
    total = both[:, :rows] + nn(panel, low_ref[...])
    total = total[:TRAITS] + total[TRAITS:]
    wide = both[:TRAITS, rows:] + both[TRAITS:, rows:]
    wide = wide + pltpu.roll(wide, HALF, 1)
    row = lax.broadcasted_iota(jnp.int32, wide.shape, 0) % 8
    lane = lax.broadcasted_iota(jnp.int32, wide.shape, 1) // TRAITS
    wide = jnp.where(row == lane, wide, 0.0)
    top = jnp.sum(wide[:8], axis=0, keepdims=True)
    bottom = jnp.sum(wide[8:], axis=0, keepdims=True)
    score = jnp.concatenate([top, bottom], axis=0)
    for y in range(Y):
        pair = packed(total[:, y * 128 : (y + 1) * 128])
        for c in range(C):
            for i in range(4):
                out_ref[y * C + c, i] = pair[c][2 * i : 2 * i + 2]
            out_ref[y * C + c, 4] = score


def own_kernel(parts_ref, own_ref, score_ref):
    total = jnp.sum(parts_ref[...], axis=0)
    for i in range(4):
        own_ref[2 * i : 2 * i + 2, :] = total[i]
    score_ref[...] = jnp.broadcast_to(total[4:], score_ref.shape)


def result_kernel(own_ref, parts_ref, kin_ref, score_ref, *, scale):
    own = own_ref[...]
    kin_ref[:8, :] = own[:, :HALF]
    kin_ref[8:, :] = pltpu.roll(own, HALF, 1)[:, :HALF]
    total = jnp.sum(parts_ref[...], axis=0)
    rows = [total[b // 8 : b // 8 + 1, b % 8 * TRAITS : (b % 8 + 1) * TRAITS] for b in range(TRAITS)]
    score_ref[...] = jnp.concatenate(rows, axis=0).T * scale


def shards(panel_t, kinship):
    f32 = jnp.float32
    slab_rows = kinship.shape[0]
    peers = X * Y * C
    pieces = pl.pallas_call(pack_kernel, out_shape=jax.ShapeDtypeStruct((peers, 8, 128), f32), in_specs=[VMEM], out_specs=VMEM, compiler_params=SMALL, name="pack")(panel_t)
    slab = lax.all_to_all(pieces, PLANE, 0, 0, tiled=True)
    block = lax.ppermute(slab, AXES, plane_to_column())
    high, low = pl.pallas_call(
        prepare_kernel,
        out_shape=(
            jax.ShapeDtypeStruct((kinship.shape[1], slab_rows + 8 * TRAITS), jnp.bfloat16),
            jax.ShapeDtypeStruct(kinship.shape[::-1], jnp.bfloat16),
        ),
        in_specs=[VMEM, pl.BlockSpec(memory_space=pltpu.HBM)],
        out_specs=(VMEM, VMEM),
        scratch_shapes=[pltpu.VMEM((CHUNKS, slab_rows // CHUNKS, kinship.shape[1]), f32), pltpu.SemaphoreType.DMA((CHUNKS,))],
        compiler_params=WHOLE,
        name="prepare",
    )(slab, kinship)
    parts = pl.pallas_call(
        product_kernel,
        out_shape=jax.ShapeDtypeStruct((Y * C, 5, 2, 128), f32),
        in_specs=[VMEM] * 3,
        out_specs=VMEM,
        compiler_params=LARGE,
        name="product",
    )(block, high, low)
    parts = lax.all_to_all(parts, COLS, 0, 0, tiled=True)
    own, scores = pl.pallas_call(
        own_kernel,
        out_shape=(jax.ShapeDtypeStruct((8, 128), f32), jax.ShapeDtypeStruct((Z * X, 2, 128), f32)),
        in_specs=[VMEM],
        out_specs=(VMEM, VMEM),
        compiler_params=SMALL,
        name="own",
    )(parts)
    scores = lax.all_to_all(scores, ROWS, 0, 0, tiled=True)
    samples = OWN * Z * X * Y * C
    return pl.pallas_call(
        lambda *refs: result_kernel(*refs, scale=samples**-0.5),
        out_shape=(jax.ShapeDtypeStruct(panel_t.shape, f32), jax.ShapeDtypeStruct((TRAITS, TRAITS), f32)),
        in_specs=[VMEM, VMEM],
        out_specs=(VMEM, VMEM),
        compiler_params=SMALL,
        name="result",
    )(own, scores)


def solution(mesh):
    torus = Mesh(mesh.devices.reshape(Z, X, Y, C), AXES)
    return jax.shard_map(
        shards,
        mesh=torus,
        in_specs=(P(None, AXES), P(ROWS, COLS)),
        out_specs=(P(None, AXES), P()),
        check_vma=False,
    )
```

```python
import jax
import jax.numpy as jnp
from jax import lax
from jax.experimental import pallas as pl
from jax.experimental.pallas import tpu as pltpu
from jax.sharding import Mesh
from jax.sharding import PartitionSpec as P

Z, X, Y, C = 8, 4, 4, 2
AXES = ("z", "x", "y", "c")
ROWS = ("z", "x")
COLS = ("y", "c")
PLANE = ("x", "y", "c")
TRAITS = 16
OWN = 64
CHUNKS = 4
HALF = 64
VMEM = pl.BlockSpec(memory_space=pltpu.VMEM)
SMALL = pltpu.CompilerParams(vmem_limit_bytes=2 << 20)
LARGE = pltpu.CompilerParams(vmem_limit_bytes=16 << 20)
WHOLE = pltpu.CompilerParams(vmem_limit_bytes=48 << 20)


def number(z, x, y, c):
    return ((z * X + x) * Y + y) * C + c


SENDER = (
    (6, 3, 5, 1, 0, 2, 4, 7),
    (4, 5, 2, 3, 7, 1, 6, 0),
    (1, 7, 0, 6, 2, 4, 3, 5),
    (2, 0, 5, 7, 4, 6, 1, 3),
    (4, 7, 0, 3, 1, 2, 6, 5),
    (2, 5, 3, 4, 1, 6, 0, 7),
    (0, 6, 7, 1, 5, 3, 4, 2),
    (3, 0, 4, 6, 7, 5, 1, 2),
)


def plane_to_column():
    return [
        (number(p, x, *divmod(SENDER[p][z], C)), number(z, x, *divmod(p, C))) for p in range(Z) for x in range(X) for z in range(Z)
    ]


def low_lanes(shape):
    return lax.broadcasted_iota(jnp.int32, shape, len(shape) - 1) < HALF


def unpacked(a, b):
    low = low_lanes(a.shape)
    top = jnp.where(low, a, pltpu.roll(b, HALF, 1))
    bottom = jnp.where(low, pltpu.roll(a, HALF, 1), b)
    return jnp.concatenate([top, bottom], axis=0)


def packed(tile):
    top, bottom = tile[:8], tile[8:]
    low = low_lanes(top.shape)
    return jnp.where(low, top, pltpu.roll(bottom, HALF, 1)), jnp.where(low, pltpu.roll(top, HALF, 1), bottom)


def split(x):
    high = x.astype(jnp.bfloat16)
    return high, (x - high.astype(jnp.float32)).astype(jnp.bfloat16)


def nn(left, right):
    return lax.dot_general(left, right, (((1,), (0,)), ((), ())), preferred_element_type=jnp.float32)


def pack_kernel(panel_ref, out_ref):
    panel = panel_ref[...]
    piece = jnp.concatenate([panel[:8], panel[8:]], axis=1)
    out_ref[...] = jnp.broadcast_to(piece[None], out_ref.shape)


def prepare_kernel(slab_ref, kinship_ref, high_ref, low_ref, buffer, sems):
    rows = kinship_ref.shape[0]
    height = rows // CHUNKS

    def copy(i):
        return pltpu.make_async_copy(kinship_ref.at[pl.ds(i * height, height)], buffer.at[i], sems.at[i])

    for i in range(CHUNKS):
        copy(i).start()
    start = lax.axis_index("x") * (Y * C)
    own = jnp.concatenate([unpacked(slab_ref[start + j], slab_ref[start + j + 1]) for j in range(0, Y * C, 2)], axis=1)
    own = jnp.concatenate(split(own), axis=0)
    form = jnp.zeros((2 * TRAITS, kinship_ref.shape[1]), jnp.float32)
    for i in range(CHUNKS):
        copy(i).wait()
        across = slice(i * height, (i + 1) * height)
        high_ref[:, across], low_ref[:, across] = split(buffer[i].T)
        for part in split(buffer[i]):
            form = form + nn(own[:, across], part)
    form = form[:TRAITS] + form[TRAITS:]
    high, low = (part.astype(jnp.float32) for part in split(form))
    high_ref[:, rows:] = jnp.concatenate([high] * 4 + [low] * 4, axis=0).T.astype(jnp.bfloat16)


def product_kernel(block_ref, high_ref, low_ref, out_ref):
    tiles = [unpacked(block_ref[j], block_ref[j + 1]) for j in range(0, block_ref.shape[0], 2)]
    panel = jnp.concatenate(split(jnp.concatenate(tiles, axis=1)), axis=0)
    rows = low_ref.shape[1]
    both = nn(panel, high_ref[...])
    total = both[:, :rows] + nn(panel, low_ref[...])
    total = total[:TRAITS] + total[TRAITS:]
    wide = both[:TRAITS, rows:] + both[TRAITS:, rows:]
    wide = wide + pltpu.roll(wide, HALF, 1)
    row = lax.broadcasted_iota(jnp.int32, wide.shape, 0) % 8
    lane = lax.broadcasted_iota(jnp.int32, wide.shape, 1) // TRAITS
    wide = jnp.where(row == lane, wide, 0.0)
    top = jnp.sum(wide[:8], axis=0, keepdims=True)
    bottom = jnp.sum(wide[8:], axis=0, keepdims=True)
    score = jnp.concatenate([top, bottom], axis=0)
    for y in range(Y):
        pair = packed(total[:, y * 128 : (y + 1) * 128])
        for c in range(C):
            for i in range(4):
                out_ref[y * C + c, i] = pair[c][2 * i : 2 * i + 2]
            out_ref[y * C + c, 4] = score


def own_kernel(parts_ref, own_ref, score_ref):
    total = jnp.sum(parts_ref[...], axis=0)
    for i in range(4):
        own_ref[2 * i : 2 * i + 2, :] = total[i]
    score_ref[...] = jnp.broadcast_to(total[4:], score_ref.shape)


def result_kernel(own_ref, parts_ref, kin_ref, score_ref, *, scale):
    own = own_ref[...]
    kin_ref[:8, :] = own[:, :HALF]
    kin_ref[8:, :] = pltpu.roll(own, HALF, 1)[:, :HALF]
    total = jnp.sum(parts_ref[...], axis=0)
    rows = [total[b // 8 : b // 8 + 1, b % 8 * TRAITS : (b % 8 + 1) * TRAITS] for b in range(TRAITS)]
    score_ref[...] = jnp.concatenate(rows, axis=0).T * scale


def shards(panel_t, kinship):
    f32 = jnp.float32
    slab_rows = kinship.shape[0]
    peers = X * Y * C
    pieces = pl.pallas_call(pack_kernel, out_shape=jax.ShapeDtypeStruct((peers, 8, 128), f32), in_specs=[VMEM], out_specs=VMEM, compiler_params=SMALL, name="pack")(panel_t)
    slab = lax.all_to_all(pieces, PLANE, 0, 0, tiled=True)
    block = lax.ppermute(slab, AXES, plane_to_column())
    high, low = pl.pallas_call(
        prepare_kernel,
        out_shape=(
            jax.ShapeDtypeStruct((kinship.shape[1], slab_rows + 8 * TRAITS), jnp.bfloat16),
            jax.ShapeDtypeStruct(kinship.shape[::-1], jnp.bfloat16),
        ),
        in_specs=[VMEM, pl.BlockSpec(memory_space=pltpu.HBM)],
        out_specs=(VMEM, VMEM),
        scratch_shapes=[pltpu.VMEM((CHUNKS, slab_rows // CHUNKS, kinship.shape[1]), f32), pltpu.SemaphoreType.DMA((CHUNKS,))],
        compiler_params=WHOLE,
        name="prepare",
    )(slab, kinship)
    parts = pl.pallas_call(
        product_kernel,
        out_shape=jax.ShapeDtypeStruct((Y * C, 5, 2, 128), f32),
        in_specs=[VMEM] * 3,
        out_specs=VMEM,
        compiler_params=LARGE,
        name="product",
    )(block, high, low)
    parts = lax.all_to_all(parts, COLS, 0, 0, tiled=True)
    own, scores = pl.pallas_call(
        own_kernel,
        out_shape=(jax.ShapeDtypeStruct((8, 128), f32), jax.ShapeDtypeStruct((Z * X, 2, 128), f32)),
        in_specs=[VMEM],
        out_specs=(VMEM, VMEM),
        compiler_params=SMALL,
        name="own",
    )(parts)
    scores = lax.all_to_all(scores, ROWS, 0, 0, tiled=True)
    samples = OWN * Z * X * Y * C
    return pl.pallas_call(
        lambda *refs: result_kernel(*refs, scale=samples**-0.5),
        out_shape=(jax.ShapeDtypeStruct(panel_t.shape, f32), jax.ShapeDtypeStruct((TRAITS, TRAITS), f32)),
        in_specs=[VMEM, VMEM],
        out_specs=(VMEM, VMEM),
        compiler_params=SMALL,
        name="result",
    )(own, scores)


def solution(mesh):
    torus = Mesh(mesh.devices.reshape(Z, X, Y, C), AXES)
    return jax.shard_map(
        shards,
        mesh=torus,
        in_specs=(P(None, AXES), P(ROWS, COLS)),
        out_specs=(P(None, AXES), P()),
        check_vma=False,
    )
```

```python
import jax
import jax.numpy as jnp
from jax import lax
from jax.experimental import pallas as pl
from jax.experimental.pallas import tpu as pltpu
from jax.sharding import Mesh
from jax.sharding import PartitionSpec as P

Z, X, Y, C = 8, 4, 4, 2
AXES = ("z", "x", "y", "c")
ROWS = ("z", "x")
COLS = ("y", "c")
PLANE = ("x", "y", "c")
TRAITS = 16
OWN = 64
CHUNKS = 4
HALF = 64
VMEM = pl.BlockSpec(memory_space=pltpu.VMEM)
SMALL = pltpu.CompilerParams(vmem_limit_bytes=2 << 20)
LARGE = pltpu.CompilerParams(vmem_limit_bytes=16 << 20)
WHOLE = pltpu.CompilerParams(vmem_limit_bytes=48 << 20)


def number(z, x, y, c):
    return ((z * X + x) * Y + y) * C + c


SENDER = (
    (4, 6, 3, 0, 1, 2, 7, 5),
    (7, 4, 5, 2, 6, 1, 0, 3),
    (1, 0, 6, 7, 4, 3, 2, 5),
    (3, 0, 1, 7, 6, 4, 5, 2),
    (5, 4, 2, 3, 0, 1, 6, 7),
    (3, 4, 5, 2, 7, 0, 1, 6),
    (1, 5, 7, 6, 4, 0, 3, 2),
    (3, 1, 4, 7, 6, 0, 5, 2),
)


def plane_to_column():
    return [
        (number(p, x, *divmod(SENDER[p][z], C)), number(z, x, *divmod(p, C))) for p in range(Z) for x in range(X) for z in range(Z)
    ]


def low_lanes(shape):
    return lax.broadcasted_iota(jnp.int32, shape, len(shape) - 1) < HALF


def unpacked(a, b):
    low = low_lanes(a.shape)
    top = jnp.where(low, a, pltpu.roll(b, HALF, 1))
    bottom = jnp.where(low, pltpu.roll(a, HALF, 1), b)
    return jnp.concatenate([top, bottom], axis=0)


def packed(tile):
    top, bottom = tile[:8], tile[8:]
    low = low_lanes(top.shape)
    return jnp.where(low, top, pltpu.roll(bottom, HALF, 1)), jnp.where(low, pltpu.roll(top, HALF, 1), bottom)


def split(x):
    high = x.astype(jnp.bfloat16)
    return high, (x - high.astype(jnp.float32)).astype(jnp.bfloat16)


def nn(left, right):
    return lax.dot_general(left, right, (((1,), (0,)), ((), ())), preferred_element_type=jnp.float32)


def pack_kernel(panel_ref, out_ref):
    panel = panel_ref[...]
    piece = jnp.concatenate([panel[:8], panel[8:]], axis=1)
    out_ref[...] = jnp.broadcast_to(piece[None], out_ref.shape)


def prepare_kernel(slab_ref, kinship_ref, high_ref, low_ref, buffer, sems):
    rows = kinship_ref.shape[0]
    height = rows // CHUNKS

    def copy(i):
        return pltpu.make_async_copy(kinship_ref.at[pl.ds(i * height, height)], buffer.at[i], sems.at[i])

    for i in range(CHUNKS):
        copy(i).start()
    start = lax.axis_index("x") * (Y * C)
    own = jnp.concatenate([unpacked(slab_ref[start + j], slab_ref[start + j + 1]) for j in range(0, Y * C, 2)], axis=1)
    own = jnp.concatenate(split(own), axis=0)
    form = jnp.zeros((2 * TRAITS, kinship_ref.shape[1]), jnp.float32)
    for i in range(CHUNKS):
        copy(i).wait()
        across = slice(i * height, (i + 1) * height)
        high_ref[:, across], low_ref[:, across] = split(buffer[i].T)
        for part in split(buffer[i]):
            form = form + nn(own[:, across], part)
    form = form[:TRAITS] + form[TRAITS:]
    high, low = (part.astype(jnp.float32) for part in split(form))
    high_ref[:, rows:] = jnp.concatenate([high] * 4 + [low] * 4, axis=0).T.astype(jnp.bfloat16)


def product_kernel(block_ref, high_ref, low_ref, out_ref):
    tiles = [unpacked(block_ref[j], block_ref[j + 1]) for j in range(0, block_ref.shape[0], 2)]
    panel = jnp.concatenate(split(jnp.concatenate(tiles, axis=1)), axis=0)
    rows = low_ref.shape[1]
    both = nn(panel, high_ref[...])
    total = both[:, :rows] + nn(panel, low_ref[...])
    total = total[:TRAITS] + total[TRAITS:]
    wide = both[:TRAITS, rows:] + both[TRAITS:, rows:]
    wide = wide + pltpu.roll(wide, HALF, 1)
    row = lax.broadcasted_iota(jnp.int32, wide.shape, 0) % 8
    lane = lax.broadcasted_iota(jnp.int32, wide.shape, 1) // TRAITS
    wide = jnp.where(row == lane, wide, 0.0)
    top = jnp.sum(wide[:8], axis=0, keepdims=True)
    bottom = jnp.sum(wide[8:], axis=0, keepdims=True)
    score = jnp.concatenate([top, bottom], axis=0)
    for y in range(Y):
        pair = packed(total[:, y * 128 : (y + 1) * 128])
        for c in range(C):
            for i in range(4):
                out_ref[y * C + c, i] = pair[c][2 * i : 2 * i + 2]
            out_ref[y * C + c, 4] = score


def own_kernel(parts_ref, own_ref, score_ref):
    total = jnp.sum(parts_ref[...], axis=0)
    for i in range(4):
        own_ref[2 * i : 2 * i + 2, :] = total[i]
    score_ref[...] = jnp.broadcast_to(total[4:], score_ref.shape)


def result_kernel(own_ref, parts_ref, kin_ref, score_ref, *, scale):
    own = own_ref[...]
    kin_ref[:8, :] = own[:, :HALF]
    kin_ref[8:, :] = pltpu.roll(own, HALF, 1)[:, :HALF]
    total = jnp.sum(parts_ref[...], axis=0)
    rows = [total[b // 8 : b // 8 + 1, b % 8 * TRAITS : (b % 8 + 1) * TRAITS] for b in range(TRAITS)]
    score_ref[...] = jnp.concatenate(rows, axis=0).T * scale


def shards(panel_t, kinship):
    f32 = jnp.float32
    slab_rows = kinship.shape[0]
    peers = X * Y * C
    pieces = pl.pallas_call(pack_kernel, out_shape=jax.ShapeDtypeStruct((peers, 8, 128), f32), in_specs=[VMEM], out_specs=VMEM, compiler_params=SMALL, name="pack")(panel_t)
    slab = lax.all_to_all(pieces, PLANE, 0, 0, tiled=True)
    block = lax.ppermute(slab, AXES, plane_to_column())
    high, low = pl.pallas_call(
        prepare_kernel,
        out_shape=(
            jax.ShapeDtypeStruct((kinship.shape[1], slab_rows + 8 * TRAITS), jnp.bfloat16),
            jax.ShapeDtypeStruct(kinship.shape[::-1], jnp.bfloat16),
        ),
        in_specs=[VMEM, pl.BlockSpec(memory_space=pltpu.HBM)],
        out_specs=(VMEM, VMEM),
        scratch_shapes=[pltpu.VMEM((CHUNKS, slab_rows // CHUNKS, kinship.shape[1]), f32), pltpu.SemaphoreType.DMA((CHUNKS,))],
        compiler_params=WHOLE,
        name="prepare",
    )(slab, kinship)
    parts = pl.pallas_call(
        product_kernel,
        out_shape=jax.ShapeDtypeStruct((Y * C, 5, 2, 128), f32),
        in_specs=[VMEM] * 3,
        out_specs=VMEM,
        compiler_params=LARGE,
        name="product",
    )(block, high, low)
    parts = lax.all_to_all(parts, COLS, 0, 0, tiled=True)
    own, scores = pl.pallas_call(
        own_kernel,
        out_shape=(jax.ShapeDtypeStruct((8, 128), f32), jax.ShapeDtypeStruct((Z * X, 2, 128), f32)),
        in_specs=[VMEM],
        out_specs=(VMEM, VMEM),
        compiler_params=SMALL,
        name="own",
    )(parts)
    scores = lax.all_to_all(scores, ROWS, 0, 0, tiled=True)
    samples = OWN * Z * X * Y * C
    return pl.pallas_call(
        lambda *refs: result_kernel(*refs, scale=samples**-0.5),
        out_shape=(jax.ShapeDtypeStruct(panel_t.shape, f32), jax.ShapeDtypeStruct((TRAITS, TRAITS), f32)),
        in_specs=[VMEM, VMEM],
        out_specs=(VMEM, VMEM),
        compiler_params=SMALL,
        name="result",
    )(own, scores)


def solution(mesh):
    torus = Mesh(mesh.devices.reshape(Z, X, Y, C), AXES)
    return jax.shard_map(
        shards,
        mesh=torus,
        in_specs=(P(None, AXES), P(ROWS, COLS)),
        out_specs=(P(None, AXES), P()),
        check_vma=False,
    )
```
